32 devices in a mesh: col: 16 (over z, x, core), row: 2 (over y).
Axes of the slice: x: 2, y: 2, z: 4, core: 2. Of those that a mesh axis runs over, the one named last changes fastest.
Arguments:
- uniq_rows: bfloat16 [32, 128, 1536], P('row', 'col'), may hold values from -6 to 6
- row_ids: int32 [32, 128, 8], P('row', 'col'), may hold values from 0 to 255, as said below
- sample_idx: int32 [512, 128], P('row', 'col'), may hold values from 0 to 7, as said below
- fm_proj: bfloat16 [128, 8], replicated, may hold values from -0.5 to 0.5
- ln_gain: float32 [1024], replicated, may hold values from 0.5 to 1.5
- w_up: bfloat16 [1024, 2048], P(None, 'row'), may hold values from -0.1875 to 0.1875
- w_down: bfloat16 [2048, 1536], P('row'), may hold values from -0.125 to 0.125
- w_lc: bfloat16 [8, 128], replicated, may hold values from -0.5 to 0.5
- w_res: bfloat16 [16, 128], replicated, may hold values from -0.5 to 0.5
- out_gain: float32 [192], replicated, may hold values from 0.5 to 1.5
- cotangent: bfloat16 [512, 3072], P(('row', 'col')), may hold values from -6 to 6
- moment1: float32 [128, 256, 192], P('col', 'row'), may hold values from -1.5 to 1.5
- moment2: float32 [128, 256], P('col', 'row'), may hold values from 0.01 to 0.1
Outputs:
- layer_out: bfloat16 [512, 3072], P(('row', 'col'))
- new_moment1: float32 [128, 256, 192], P('col', 'row')
- new_moment2: float32 [128, 256], P('col', 'row')
- row_step: float32 [128, 256, 192], P('col', 'row')
The draws below stay inside these ranges and needn't reach their ends.
Inputs may be any that keep to these rules, and one draw needn't show every extreme that they name: `sample_idx`: for each block of 16 samples and each slot, every one of the 8 list entries is used by at least one sample of the block. `row_ids`: the 8 ids of one list are distinct. Row v of a slot is owned by index v // 128 of row. Of the 1024 list entries held by one device (the blocks of its index of row, the slots of its index of col), at most 640 name rows of one owner, and in every draw some owner is named exactly 640 times on each device.
All inputs are finite; a program needn't handle non-finite values.
Results may differ from the reference program's by a relative error of at most 0.005.
Values may be sent and summed in bfloat16 or wider, within the bound.
A program may use at most 64 MiB of HBM per device.

```python
import math
import jax
import jax.numpy as jnp
from jax import lax

SLOTS = 128
E = 192
RANK = 8
HID = 2048
NF = 8
NL = 8
S_DEV = 16
V_DEV = 128
UNIQ = 8
SLOTS_DEV = 8
FLAT = 1024
NOUT = 16
NBLK = 32
SAMPLES = 512
VOCAB = 256
CAP = 640
N_COL = 16
N_ROW = 2


def draw_sample_idx(key, part):
    first, second = jax.random.split(key)
    filler = jax.random.randint(first, (NBLK, SLOTS, S_DEV), 0, UNIQ)
    scores = jax.random.randint(second, (NBLK, SLOTS, S_DEV), 0, 1 << 20) * S_DEV + jnp.arange(S_DEV, dtype=jnp.int32)
    order = jnp.argsort(scores, axis=-1)
    ranks = jnp.argsort(order, axis=-1).astype(jnp.int32)
    chosen = jnp.where(ranks < UNIQ, ranks, filler)
    return jnp.transpose(chosen, (0, 2, 1)).reshape(SAMPLES, SLOTS)


def draw_row_ids(key, part):
    keys = jax.random.split(key, 4)
    entries = SLOTS * UNIQ
    rest = entries - CAP
    share = rest // (N_ROW - 1)
    extra = rest % (N_ROW - 1)
    relative_owner = jnp.arange(N_ROW, dtype=jnp.int32)
    counts = jnp.where(relative_owner == 0, CAP, share + (relative_owner - 1 < extra).astype(jnp.int32))
    bounds = jnp.cumsum(counts)
    position = jnp.arange(entries, dtype=jnp.int32)
    relative = jnp.sum((position[:, None] >= bounds[None, :]).astype(jnp.int32), 1)
    busiest = jax.random.randint(keys[0], (N_COL,), 0, N_ROW)
    ordered = (relative[None, :] + busiest[:, None]) % N_ROW
    scores = jax.random.randint(keys[1], (N_ROW, N_COL, entries), 0, 1 << 16) * entries + position
    shuffle = jnp.argsort(scores, axis=-1)
    owner = jnp.take_along_axis(jnp.broadcast_to(ordered[None], (N_ROW, N_COL, entries)), shuffle, axis=-1)
    owner = owner.reshape(N_ROW, N_COL, N_COL, SLOTS_DEV, UNIQ)
    owner = jnp.transpose(owner, (0, 2, 1, 3, 4)).reshape(NBLK, SLOTS, UNIQ)
    offset = jax.random.randint(keys[2], (NBLK, SLOTS, 1), 0, V_DEV)
    stride = 2 * jax.random.randint(keys[3], (NBLK, SLOTS, 1), 0, max(V_DEV // 2, 1)) + 1
    local = (offset + jnp.arange(UNIQ, dtype=jnp.int32) * stride) % V_DEV
    return (owner * V_DEV + local).astype(jnp.int32)


def levels(rng, extent, pieces, smallest, high):
    def one(dim, shards_of):
        draws = jax.random.uniform(jax.random.fold_in(jax.random.fold_in(rng, 6), dim), (shards_of,), jnp.float32, smallest / len(pieces), high / len(pieces))
        return jnp.repeat(jnp.exp(draws), extent[dim] // shards_of).reshape((-1,) + (1,) * (len(extent) - dim - 1))

    level = one(*pieces[0])
    for cut in pieces[1:]:
        level = level * one(*cut)
    return level


def gaussian(stream_key, dims, width, reach, cuts=(), held_as=jnp.bfloat16):
    level = levels(stream_key, dims, cuts, -0.22, 0.18) if cuts else 1.0
    drawn = jax.random.normal(stream_key, dims, jnp.float32) * width * level
    return jnp.minimum(jnp.maximum(drawn, -reach), reach).astype(held_as)


def setup_inputs(seed: int = 0) -> dict:
    key_list = jax.random.split(jax.random.key(seed), 14)
    return {
        "uniq_rows": gaussian(key_list[0], (NBLK, SLOTS, UNIQ * E), 1.0, 6.0, ((0, 2), (1, 16))),
        "row_ids": draw_row_ids(jax.random.fold_in(key_list[13], 71), 0),
        "sample_idx": draw_sample_idx(jax.random.fold_in(key_list[13], 71), 0),
        "fm_proj": gaussian(key_list[3], (SLOTS, RANK), SLOTS ** -0.5, 0.5),
        "ln_gain": jnp.clip(1.0 + 0.1 * jax.random.normal(key_list[4], (FLAT,), jnp.float32), 0.5, 1.5),
        "w_up": gaussian(key_list[5], (FLAT, HID), FLAT ** -0.5, 0.1875, ((1, 2),)),
        "w_down": gaussian(key_list[6], (HID, NF * E), HID ** -0.5, 0.125, ((0, 2),)),
        "w_lc": gaussian(key_list[7], (NL, SLOTS), SLOTS ** -0.5, 0.5),
        "w_res": gaussian(key_list[8], (NOUT, SLOTS), SLOTS ** -0.5, 0.5),
        "out_gain": jnp.clip(1.0 + 0.1 * jax.random.normal(key_list[9], (E,), jnp.float32), 0.5, 1.5),
        "cotangent": gaussian(key_list[10], (SAMPLES, NOUT * E), 1.0, 6.0, ((0, 32),)),
        "moment1": gaussian(key_list[11], (SLOTS, VOCAB, E), 0.1, 1.5, ((0, 16), (1, 2)), jnp.float32),
        "moment2": jnp.clip(jnp.exp(math.log(0.1) - 2.3025851 * jax.random.uniform(key_list[12], (SLOTS, VOCAB), jnp.float32) ** levels(key_list[12], (SLOTS, VOCAB), ((0, 16), (1, 2)), -0.2, 0.2)), 0.01, 0.1),
    }


HIGH = lax.Precision.HIGHEST

def layer_norm(values, gain):
    centered = values - lax.optimization_barrier(jnp.mean(values, -1, keepdims=True))
    inverse = lax.rsqrt(lax.optimization_barrier(jnp.mean(centered * centered, -1, keepdims=True)) + 1e-05)
    normed = centered * inverse
    return (normed * gain, normed, inverse)

def norm_back(grad_out, normed, inverse):
    first = lax.optimization_barrier(jnp.mean(grad_out, -1, keepdims=True))
    second = lax.optimization_barrier(jnp.mean(grad_out * normed, -1, keepdims=True))
    return (grad_out - first - normed * second) * inverse

def silu_grad(values):
    sigma = jax.nn.sigmoid(values)
    return sigma * (1.0 + values * (1.0 - sigma))

def block_step(embed, cotangent, fm_proj, ln_gain, w_up, w_down, w_lc, w_res, out_gain):
    count = embed.shape[0]
    embed32 = embed.astype(jnp.float32)
    proj32 = fm_proj.astype(jnp.float32)
    lc32 = w_lc.astype(jnp.float32)
    res32 = w_res.astype(jnp.float32)
    compress = jnp.einsum('ste,tk->sek', embed32, proj32, precision=HIGH).astype(jnp.bfloat16)
    comp32 = compress.astype(jnp.float32)
    gram = jnp.einsum('ste,sek->stk', embed32, comp32, precision=HIGH)
    flat = gram.reshape(count, FLAT)
    scaled, normed_in, inverse_in = layer_norm(flat, ln_gain)
    normal_in = scaled.astype(jnp.bfloat16)
    hidden_pre = jnp.dot(normal_in, w_up, preferred_element_type=jnp.float32)
    hidden = jax.nn.silu(hidden_pre).astype(jnp.bfloat16)
    fm_out = jnp.dot(hidden, w_down, preferred_element_type=jnp.float32)
    linear = jnp.einsum('lt,ste->sle', lc32, embed32, precision=HIGH)
    joined = jnp.concatenate([fm_out.reshape(count, NF, E), linear], 1)
    normed_out, normed_rows, inverse_rows = layer_norm(joined, out_gain)
    residual = jnp.einsum('ot,ste->soe', res32, embed32, precision=HIGH)
    result = (normed_out + residual).reshape(count, NOUT * E).astype(jnp.bfloat16)
    upstream = cotangent.astype(jnp.float32).reshape(count, NOUT, E)
    grad_joined = norm_back(upstream * out_gain, normed_rows, inverse_rows)
    grad_fm = grad_joined[:, :NF].reshape(count, NF * E).astype(jnp.bfloat16)
    grad_hidden = lax.dot_general(grad_fm, w_down, (((1,), (1,)), ((), ())), preferred_element_type=jnp.float32)
    grad_pre = (grad_hidden * silu_grad(hidden_pre)).astype(jnp.bfloat16)
    grad_flat = lax.dot_general(grad_pre, w_up, (((1,), (1,)), ((), ())), preferred_element_type=jnp.float32)
    grad_gram = norm_back(grad_flat * ln_gain, normed_in, inverse_in).reshape(count, SLOTS, RANK)
    grad_embed = jnp.einsum('stk,sek->ste', grad_gram, comp32, precision=HIGH)
    grad_comp = jnp.einsum('ste,stk->sek', embed32, grad_gram, precision=HIGH)
    grad_embed = grad_embed + jnp.einsum('tk,sek->ste', proj32, grad_comp, precision=HIGH)
    grad_embed = grad_embed + jnp.einsum('lt,sle->ste', lc32, grad_joined[:, NF:], precision=HIGH)
    grad_embed = grad_embed + jnp.einsum('ot,soe->ste', res32, upstream, precision=HIGH)
    return (result, grad_embed)

def reference(uniq_rows, row_ids, sample_idx, fm_proj, ln_gain, w_up, w_down, w_lc, w_res, out_gain, cotangent, moment1, moment2):
    rows = uniq_rows.reshape(NBLK, SLOTS, UNIQ, E)
    index = sample_idx.reshape(NBLK, S_DEV, SLOTS)
    upstream = cotangent.reshape(NBLK, S_DEV, NOUT * E)
    slot_row = jnp.arange(SLOTS, dtype=jnp.int32)[None, :]
    slot_col = jnp.arange(SLOTS, dtype=jnp.int32)[:, None]

    def visit(grads, inputs):
        block_rows, block_index, block_cot, block_ids = inputs
        embed = block_rows[slot_row, block_index]
        result, grad_embed = block_step(embed, block_cot, fm_proj, ln_gain, w_up, w_down, w_lc, w_res, out_gain)
        list_grads = jnp.zeros((SLOTS, UNIQ, E), jnp.float32).at[jnp.broadcast_to(slot_row, block_index.shape), block_index].add(grad_embed)
        grads = grads.at[jnp.broadcast_to(slot_col, block_ids.shape), block_ids].add(list_grads)
        return (grads, result)
    start = jnp.zeros((SLOTS, VOCAB, E), jnp.float32)
    row_grads, outputs = lax.scan(visit, start, (rows, index, upstream, row_ids))
    layer_out = outputs.reshape(SAMPLES, NOUT * E)
    new_moment1 = 0.9 * moment1 + 0.1 * row_grads
    new_moment2 = 0.99 * moment2 + 0.01 * lax.optimization_barrier(jnp.mean(row_grads * row_grads, -1))
    row_step = new_moment1 * lax.rsqrt(new_moment2)[..., None]
    return (layer_out, new_moment1, new_moment2, row_step)
```

```python
import functools

import jax
import jax.numpy as jnp
from jax import lax
from jax.experimental import pallas as pl
from jax.experimental.pallas import tpu as pltpu
from jax.sharding import PartitionSpec as P

HIGH = lax.Precision.HIGHEST


def layer_norm(values, gain):
    centered = values - jnp.mean(values, -1, keepdims=True)
    inverse = lax.rsqrt(jnp.mean(centered * centered, -1, keepdims=True) + 1e-05)
    normed = centered * inverse
    return (normed * gain, normed, inverse)


def norm_back(grad_out, normed, inverse):
    first = jnp.mean(grad_out, -1, keepdims=True)
    second = jnp.mean(grad_out * normed, -1, keepdims=True)
    return (grad_out - first - normed * second) * inverse


def silu_grad(values):
    sigma = jax.nn.sigmoid(values)
    return sigma * (1.0 + values * (1.0 - sigma))


def plain_body(
    uniq_rows,
    row_ids,
    sample_idx,
    fm_proj,
    ln_gain,
    w_up,
    w_down,
    w_lc,
    w_res,
    out_gain,
    cotangent,
    moment1,
    moment2,
):
    columns = lax.axis_size("col")
    owners = lax.axis_size("row")
    slot_dev = uniq_rows.shape[1]
    width = out_gain.shape[0]
    uniq = uniq_rows.shape[2] // width
    samples = cotangent.shape[0]
    slots = slot_dev * columns
    vocab_dev = moment2.shape[1]
    rank = fm_proj.shape[1]
    fm_rows = w_down.shape[1] // width
    out_rows = w_res.shape[0]
    entry_iota = jnp.arange(uniq, dtype=jnp.int32)
    index_local = sample_idx.reshape(columns, samples, slot_dev)
    index = lax.all_to_all(index_local, "col", split_axis=0, concat_axis=2, tiled=True).reshape(
        samples, slots
    )
    picker = (index[:, :, None] == entry_iota).astype(jnp.bfloat16)
    moved = lax.all_to_all(uniq_rows, "col", split_axis=0, concat_axis=1, tiled=True)
    table = moved.reshape(slots, uniq, width)
    embed = jnp.einsum("stl,tle->ste", picker, table, preferred_element_type=jnp.float32).astype(
        jnp.bfloat16
    )
    compress = jnp.einsum("ste,tk->sek", embed, fm_proj, preferred_element_type=jnp.float32).astype(
        jnp.bfloat16
    )
    gram = jnp.einsum("ste,sek->stk", embed, compress, preferred_element_type=jnp.float32)
    flat = gram.reshape(samples, slots * rank)
    scaled, normed_in, inverse_in = layer_norm(flat, ln_gain)
    normal_in = scaled.astype(jnp.bfloat16)
    hidden_pre = jnp.dot(
        lax.all_gather(normal_in, "row", axis=0, tiled=True),
        w_up,
        preferred_element_type=jnp.float32,
    )
    hidden = jax.nn.silu(hidden_pre).astype(jnp.bfloat16)
    part_rows = hidden
    fm_out = lax.psum_scatter(
        jnp.dot(part_rows, w_down, preferred_element_type=jnp.float32),
        "row",
        scatter_dimension=0,
        tiled=True,
    )
    linear = jnp.einsum("lt,ste->sle", w_lc, embed, preferred_element_type=jnp.float32)
    joined = jnp.concatenate([fm_out.reshape(samples, fm_rows, width), linear], 1)
    normed_out, normed_rows, inverse_rows = layer_norm(joined, out_gain)
    residual = jnp.einsum("ot,ste->soe", w_res, embed, preferred_element_type=jnp.float32)
    layer_out = (normed_out + residual).reshape(samples, out_rows * width).astype(jnp.bfloat16)
    upstream = cotangent.astype(jnp.float32).reshape(samples, out_rows, width)
    grad_joined = norm_back(upstream * out_gain, normed_rows, inverse_rows)
    grad_fm = grad_joined[:, :fm_rows].reshape(samples, fm_rows * width).astype(jnp.bfloat16)
    grad_hidden = lax.dot_general(
        lax.all_gather(grad_fm, "row", axis=0, tiled=True),
        w_down,
        (((1,), (1,)), ((), ())),
        preferred_element_type=jnp.float32,
    )
    grad_pre = (grad_hidden * silu_grad(hidden_pre)).astype(jnp.bfloat16)
    part_rows = grad_pre
    grad_flat = lax.psum_scatter(
        lax.dot_general(
            part_rows, w_up, (((1,), (1,)), ((), ())), preferred_element_type=jnp.float32
        ).astype(jnp.bfloat16),
        "row",
        scatter_dimension=0,
        tiled=True,
    ).astype(jnp.float32)
    grad_gram = norm_back(grad_flat * ln_gain, normed_in, inverse_in).reshape(samples, slots, rank)
    grad_embed = jnp.einsum("stk,sek->ste", grad_gram, compress.astype(jnp.float32), precision=HIGH)
    grad_comp = jnp.einsum(
        "ste,stk->sek", embed, grad_gram, precision=HIGH, preferred_element_type=jnp.float32
    )
    grad_embed = grad_embed + jnp.einsum(
        "tk,sek->ste", fm_proj.astype(jnp.float32), grad_comp, precision=HIGH
    )
    grad_embed = grad_embed + jnp.einsum(
        "lt,sle->ste", w_lc.astype(jnp.float32), grad_joined[:, fm_rows:], precision=HIGH
    )
    grad_embed = grad_embed + jnp.einsum(
        "ot,soe->ste", w_res.astype(jnp.float32), upstream, precision=HIGH
    )
    list_grads = jnp.einsum("stl,ste->tle", picker.astype(jnp.float32), grad_embed, precision=HIGH)
    returned = lax.all_to_all(
        list_grads.reshape(columns, slot_dev, uniq * width),
        "col",
        split_axis=0,
        concat_axis=0,
        tiled=True,
    )
    entry_grads = returned.reshape(columns * slot_dev * uniq, width)
    row_list = row_ids.reshape(-1)
    slot_of = jnp.broadcast_to(
        jnp.arange(slot_dev, dtype=jnp.int32)[None, :, None], row_ids.shape
    ).reshape(-1)
    owner = row_list // vocab_dev
    target = slot_of * vocab_dev + row_list % vocab_dev
    span = slot_dev * vocab_dev
    entries = row_list.shape[0]
    capacity = 5 * entries // (4 * owners)
    onehot = (owner[:, None] == jnp.arange(owners, dtype=jnp.int32)).astype(jnp.int32)
    before = jnp.cumsum(onehot, 0) - onehot
    place = jnp.sum(before * onehot, 1)
    target_slot = owner * capacity + place
    bucket = jnp.zeros((owners * capacity, width), jnp.float32).at[target_slot].set(entry_grads)
    labels = (
        jnp.full((owners * capacity,), -1.0, jnp.float32)
        .at[target_slot]
        .set(target.astype(jnp.float32))
    )
    got_rows, got_labels = (
        lax.all_to_all(
            bucket.reshape(owners, capacity, width), "row", split_axis=0, concat_axis=0, tiled=True
        ),
        lax.all_to_all(
            labels.reshape(owners, capacity), "row", split_axis=0, concat_axis=0, tiled=True
        ),
    )
    segment = jnp.where(got_labels >= 0.0, got_labels, float(span)).astype(jnp.int32).reshape(-1)
    summed = jax.ops.segment_sum(got_rows.reshape(-1, width), segment, num_segments=span + 1)[:span]
    row_grads = summed.reshape(slot_dev, vocab_dev, width)
    new_moment1 = 0.9 * moment1 + 0.1 * row_grads
    new_moment2 = 0.99 * moment2 + 0.01 * jnp.mean(row_grads * row_grads, -1)
    row_step = new_moment1 * lax.rsqrt(new_moment2)[..., None]
    return (layer_out, new_moment1, new_moment2, row_step)


F32 = jnp.float32
BF16 = jnp.bfloat16
NT = (((1,), (1,)), ((), ()))


def iota(shape, dim):
    return lax.broadcasted_iota(jnp.int32, shape, dim)


def matmul(a, b, dims=(((1,), (0,)), ((), ())), precision=None):
    return lax.dot_general(a, b, dims, precision=precision, preferred_element_type=F32)


def fused_kernel(
    C,
    D,
    uniq,
    rid_in,
    sidx_in,
    fmp_in,
    gain_in,
    wup,
    wdn,
    wlc_in,
    wres_in,
    og_in,
    cot_in,
    m1_in,
    m2_in,
    lay_out,
    rg_out,
    pr,
    m1_out,
    m2_out,
    rid,
    sidx,
    fmp,
    gain,
    wlc,
    wres,
    og,
    cot,
    cpeer,
    isend,
    land,
    iland,
    wraw,
    wp,
    wd,
    t32,
    tst,
    lm,
    lmask,
    arep,
    rmat,
    nrm,
    ggr,
    idxn,
    nall,
    y,
    ds,
    c32,
    fsend,
    frecv,
    fm,
    qsend,
    qrecv,
    gq,
    lay32,
    gf32,
    lge,
    sb,
    rland,
    oh,
    ps,
    loc,
    s1,
    r1,
    si,
    ri,
    su,
    ru,
    sx,
    rx,
):
    S, E, U, K, T = 16, 192, 8, 8, 128
    FC, QC = 3, 2
    me = lax.axis_index("col")
    mr = lax.axis_index("row")
    other = 1 - mr

    def to_col(i):
        return lax.rem(me + i, C)

    def rcopy(src, dst, ssem, rsem, where):
        return pltpu.make_async_remote_copy(
            src_ref=src,
            dst_ref=dst,
            send_sem=ssem,
            recv_sem=rsem,
            device_id=where,
            device_id_type=pl.DeviceIdType.MESH,
        )

    def row_send(src, dst, sem):
        copy = rcopy(src, dst, sx.at[sem], rx.at[sem], {"row": other})
        copy.start()
        return copy

    barrier = pltpu.get_barrier_semaphore()
    for i in range(1, C):
        pl.semaphore_signal(
            barrier, inc=1, device_id={"col": to_col(i)}, device_id_type=pl.DeviceIdType.MESH
        )
    pl.semaphore_signal(
        barrier, inc=1, device_id={"row": other}, device_id_type=pl.DeviceIdType.MESH
    )
    cp_idx = pltpu.make_async_copy(sidx_in, sidx, loc.at[0])
    cp_idx.start()
    cp_up = pltpu.make_async_copy(wup, wraw, loc.at[1])
    cp_dn = pltpu.make_async_copy(wdn, wd, loc.at[2])
    own_rows = pltpu.make_async_copy(uniq.at[me], land.at[me], loc.at[3])
    own_rows.start()
    small = [
        pltpu.make_async_copy(a, b, loc.at[4 + n])
        for n, (a, b) in enumerate(
            (
                (rid_in, rid),
                (fmp_in, fmp),
                (gain_in, gain),
                (wlc_in, wlc),
                (wres_in, wres),
                (og_in, og),
                (cot_in, cot),
                (m2_in, m2_out),
            )
        )
    ]
    for cp in small:
        cp.start()
    cp_m1 = pltpu.make_async_copy(m1_in, m1_out, loc.at[12])
    cp_up.start()
    cp_dn.start()
    cp_m1.start()
    cp_idx.wait()
    for p in range(C):
        at = p * S % T
        tile = sidx[:, p * S // T * T : (p * S // T + 1) * T]
        if at:
            tile = pltpu.roll(tile, T - at, 1)
        isend[p] = tile[:, :S]
    iland[me] = isend[me]
    pl.semaphore_wait(barrier, C)

    order = sorted(range(1, C), key=lambda i: -min(i, C - i))
    idx_copies, row_copies = [], []
    for i in order:
        p = to_col(i)
        idx_copies.append(rcopy(isend.at[p], iland.at[me], si.at[i], ri.at[i], {"col": p}))
        idx_copies[-1].start()
    for i in order:
        p = to_col(i)
        row_copies.append(rcopy(uniq.at[p], land.at[me], s1.at[i], r1.at[i], {"col": p}))
        row_copies[-1].start()
    c_copy = row_send(cot_in.at[:, pl.ds(0, 8 * E)], cpeer, 0)

    to, at = iota((256, 256), 0), iota((256, 256), 1)
    perm = (((to & 31) * 8 + (to >> 5)) == at).astype(F32).astype(BF16)
    for cp in small:
        cp.wait()
    cp_up.wait()
    for g in range(4):
        blk = matmul(perm, wraw[g * 256 : (g + 1) * 256, :]).astype(BF16)
        for k in range(K):
            wp[k * T + g * 32 : k * T + (g + 1) * 32, :] = blk[k * 32 : (k + 1) * 32, :]
    lane = iota((K, K * T), 1)
    spread = jnp.where((lane & 7) == iota((K, K * T), 0), gain[...], 0.0)
    fold = ((iota((K * T, T), 0) >> 3) == iota((K * T, T), 1)).astype(F32)
    gk = matmul(spread, fold, precision=HIGH)

    amat = jnp.concatenate(
        [
            fmp[...].astype(F32),
            wlc[...].astype(F32),
            wres[...].astype(F32),
        ],
        0,
    )
    for j in range(32):
        arep[j * S : (j + 1) * S, :] = jnp.broadcast_to(amat[j : j + 1, :], (S, T))

    place = (iota((C, T), 0) == (iota((C, T), 1) >> 3)).astype(F32)
    wide = matmul(rid[...].astype(F32).reshape(D * U, C), place, precision=HIGH).reshape(D, U, T)
    mine = iota((D, U, T), 1) == (iota((D, U, T), 2) & (U - 1))
    labels = jnp.sum(jnp.where(mine, wide, 0.0), 1).astype(jnp.int32)
    target = iota((T, T), 0)
    for i in range(2):
        local = labels - (mr if i == 0 else other) * T
        for d in range(D):
            oh[i, d] = jnp.where(
                target == jnp.broadcast_to(local[d : d + 1, :], (T, T)), 1.0, 0.0
            ).astype(BF16)

    for cp in idx_copies:
        cp.wait_recv()
    ix = iland[...].astype(F32).reshape(T, S)
    tiled = (iota((S, T), 0) == (iota((S, T), 1) & (S - 1))).astype(F32)
    idx_n = matmul(ix, tiled, precision=HIGH)
    idxn[...] = idx_n
    idx_t = idx_n.T
    for u in range(U):
        for q in range(4):
            lm[q * T : (q + 1) * T, u * T : (u + 1) * T] = jnp.where(
                idx_t == float(u), arep[q * T : (q + 1) * T, :], 0.0
            ).astype(BF16)
    entry = iota((U, T), 0).astype(F32)

    def fill(src, at):
        for t in range(0, T, 2):
            rows = [
                jnp.where(
                    jnp.broadcast_to(idxn[v : v + 1, :], (U, T)) == entry,
                    jnp.broadcast_to(src[v : v + 1, :], (U, T)),
                    0.0,
                )
                for v in (t, t + 1)
            ]
            lmask[t // D, t % D * U : (t % D + 2) * U, at * T : (at + 1) * T] = jnp.concatenate(
                rows, 0
            ).astype(BF16)

    for q in range(4):
        ggr[...] = arep[q * T : (q + 1) * T, :].T
        fill(ggr, (q + 3) & 3)
    upstream = cot[...].astype(F32)
    for o in range(16):
        rmat[(8 + o) * S : (9 + o) * S, :] = upstream[:, o * E : (o + 1) * E].astype(BF16)

    own_rows.wait()
    for cp in row_copies:
        cp.wait_recv()
    t32[...] = land[...].astype(F32).reshape(T, U * E)
    for u in range(U):
        tst[u * T : (u + 1) * T, :] = t32[:, u * E : (u + 1) * E].astype(BF16)

    comp = matmul(lm[0:T, :], tst[...]).astype(BF16)
    rmat[512:640, :] = comp
    z = matmul(comp, tst[...], NT)
    gram = jnp.where(idx_t == 0.0, z[:, 0:T], 0.0)
    for u in range(1, U):
        gram = gram + jnp.where(idx_t == float(u), z[:, u * T : (u + 1) * T], 0.0)
    n_flat = float(K * T)
    g3 = gram.reshape(K, S, T)
    mu = jnp.sum(jnp.sum(g3, 0), -1, keepdims=True) / n_flat
    cent = g3 - mu[None]
    inv_in = lax.rsqrt(jnp.sum(jnp.sum(cent * cent, 0), -1, keepdims=True) / n_flat + 1e-05)
    normed_in = cent * inv_in[None]
    nrm[...] = normed_in.reshape(K * S, T)
    for k in range(K):
        nall[0, :, k * T : (k + 1) * T] = (normed_in[k] * gk[k : k + 1, :]).astype(BF16)
    n_copy = row_send(nall.at[0], nall.at[1], 1)

    y[...] = matmul(lm[T:512, :], tst[...])
    gain_out = og[...]
    c_copy.wait_recv()
    c32[0:S, :] = upstream[:, 0 : 8 * E]
    c32[S : 2 * S, :] = cpeer[...].astype(F32)
    up_fm = jnp.concatenate([c32[:, o * E : (o + 1) * E] for o in range(8)], 0) * gain_out
    up_mean = jnp.mean(up_fm, -1, keepdims=True)
    cp_dn.wait()
    n_copy.wait_recv()
    hp = matmul(nall[...].reshape(2 * S, K * T), wp[...])
    sg = jax.nn.sigmoid(hp)
    hid = (hp * sg).astype(BF16)
    f_copies = []
    for c in range(FC):
        cols = slice(c * 8 * E // FC, (c + 1) * 8 * E // FC)
        fp = matmul(hid, wd[:, cols])
        fm[:, cols] = fp
        fsend[c, 0:S] = fp[S : 2 * S].astype(BF16)
        fsend[c, S : 2 * S] = fp[0:S].astype(BF16)
        f_copies.append(row_send(fsend.at[c], frecv.at[c], 2 + c))
    ds[...] = sg * (1.0 + hp * (1.0 - sg))

    def out_norm(joined, o):
        up = upstream[:, o * E : (o + 1) * E]
        c = joined - jnp.mean(joined, -1, keepdims=True)
        inv = lax.rsqrt(jnp.mean(c * c, -1, keepdims=True) + 1e-05)
        nr = c * inv
        return nr, norm_back(up * gain_out, nr, inv)

    for o in range(8, 16):
        nr, gj = out_norm(y[(o - 8) * S : (o - 7) * S, :], o)
        lay32[:, o * E : (o + 1) * E] = nr * gain_out + y[(8 + o) * S : (9 + o) * S, :]
        rmat[(o - 8) * S : (o - 7) * S, :] = gj.astype(BF16)

    for c in range(FC):
        f_copies[c].wait_recv()
        cols = slice(c * 8 * E // FC, (c + 1) * 8 * E // FC)
        fm[:, cols] += frecv[c].astype(F32)
    joined = jnp.concatenate([fm[:, o * E : (o + 1) * E] for o in range(8)], 0)
    cen = joined - jnp.mean(joined, -1, keepdims=True)
    inv_fm = lax.rsqrt(jnp.mean(cen * cen, -1, keepdims=True) + 1e-05)
    normed_fm = cen * inv_fm
    across = jnp.mean(up_fm * cen, -1, keepdims=True) * inv_fm
    grad_fm = (up_fm - up_mean - normed_fm * across) * inv_fm
    for o in range(8):
        gf32[:, o * E : (o + 1) * E] = grad_fm[o * 2 * S : (o + 1) * 2 * S]
    gh = matmul(gf32[...].astype(BF16), wd[...], NT)
    gp = (gh * ds[...]).astype(BF16)
    q_copies = []
    for c in range(QC):
        cols = slice(c * K * T // QC, (c + 1) * K * T // QC)
        part = matmul(gp, wp[cols, :], NT)
        gq[:, cols] = part[0:S]
        qsend[c] = part[S : 2 * S].astype(BF16)
        q_copies.append(row_send(qsend.at[c], qrecv.at[c], 2 + FC + c))
    for o in range(8):
        lay32[:, o * E : (o + 1) * E] = (
            normed_fm[o * 2 * S : (o * 2 + 1) * S] * gain_out + y[(8 + o) * S : (9 + o) * S, :]
        )
    lay_out[...] = lay32[...].astype(BF16)
    lge[...] = matmul(
        lmask[:, :, 0:384].reshape(C * D * U, 384), rmat[0:384, :]
    ).reshape(C, D * U, E)
    for c in range(QC):
        q_copies[c].wait_recv()
    width = K // QC
    qs = [
        (
            gq[:, k * T : (k + 1) * T]
            + qrecv[k // width, :, k % width * T : (k % width + 1) * T].astype(F32)
        )
        * gk[k : k + 1, :]
        for k in range(K)
    ]
    ns = [nrm[k * S : (k + 1) * S, :] for k in range(K)]
    first = jnp.sum(sum(qs), -1, keepdims=True) / n_flat
    second = jnp.sum(sum(q * n for q, n in zip(qs, ns)), -1, keepdims=True) / n_flat
    for k in range(K):
        ggr[k * S : (k + 1) * S, :] = (qs[k] - first - ns[k] * second) * inv_in
    gg = ggr[...]
    for u in range(U):
        lm[0:T, u * T : (u + 1) * T] = jnp.where(idx_t == float(u), gg, 0.0).astype(BF16)
    ggr[...] = gg.T
    fill(ggr, 4)
    rmat[384:512, :] = matmul(lm[0:T, :], tst[...]).astype(BF16)

    units = []
    for half in range(2):
        at = half * 32
        part = matmul(lmask[:, at : at + 32, 384:640].reshape(C * 32, 256), rmat[384:640, :])
        part = part.reshape(C, 32, E) + lge[:, at : at + 32, :]
        row = half * 48
        top = part[:, :, T:E]
        sb[:, row : row + 16, :] = jnp.concatenate([top[:, :16], top[:, 16:]], -1).astype(BF16)
        sb[:, row + 16 : row + 48, :] = part[:, :, 0:T].astype(BF16)
        for j in range(half * 3, half * 3 + 3):
            cut = pl.ds(j * 16, 16)
            units.append([])
            for i in order:
                p = to_col(i)
                sem = j * C + i
                units[j].append(
                    rcopy(sb.at[p, cut], rland.at[me, cut], su.at[sem], ru.at[sem], {"col": p})
                )
                units[j][-1].start()
    rland[me] = sb[me]

    p_copies = []
    for j in range(6):
        for cp in units[j]:
            cp.wait_recv()
        base, kind = j // 3 * 4, j % 3
        both = rland[:, j * 16 : (j + 1) * 16, :].astype(F32)
        pieces = []
        for h in range(2):
            x = both[:, h * U : (h + 1) * U, :].reshape(T, T).T.astype(BF16)
            if kind == 0:
                pieces.append((base + h, T, E, x[: E - T]))
                pieces.append((base + 2 + h, T, E, x[E - T :]))
            else:
                pieces.append((base + 2 * (kind - 1) + h, 0, T, x))
        for d, a, b, x in pieces:
            ps[d, a:b, :] = matmul(x, oh[1, d], NT).astype(BF16)
        if kind == 0:
            part = (pl.ds(base, 4), pl.ds(T, E - T))
        else:
            part = (pl.ds(base + 2 * (kind - 1), 2), pl.ds(0, T))
        p_copies.append(row_send(ps.at[part], pr.at[part], 2 + FC + QC + j))
        for d, a, b, x in pieces:
            rg_out[d, a:b, :] = matmul(x, oh[0, d], NT)
    cp_m1.wait()
    for cp in p_copies:
        cp.wait_recv()
    for group in (
        idx_copies,
        row_copies,
        [c_copy, n_copy],
        f_copies,
        q_copies,
        *units,
        p_copies,
    ):
        for cp in group:
            cp.wait_send()


def moment_kernel(
    width, lay, own, got, m1, m2, lay_out, m1_out, m2_out, step_out, mv, sv, m2v, sem
):
    D = own.shape[0]
    copies = [pltpu.make_async_copy(lay, lay_out, sem.at[0])]
    copies[0].start()
    for d in range(D):
        g = own[d] + got[d].astype(F32)
        first = 0.9 * m1[d] + 0.1 * g
        second = 0.99 * m2[d : d + 1, :] + 0.01 * (jnp.sum(g * g, 0, keepdims=True) / width)
        mv[d] = first
        m2v[d : d + 1, :] = second
        sv[d] = first * lax.rsqrt(second)
        for n, (a, b) in enumerate(((mv, m1_out), (sv, step_out))):
            copies.append(pltpu.make_async_copy(a.at[d], b.at[d], sem.at[2 + 2 * d + n]))
            copies[-1].start()
    copies.append(pltpu.make_async_copy(m2v, m2_out, sem.at[1]))
    copies[-1].start()
    for cp in copies:
        cp.wait()


def fast_body(
    C,
    R,
    uniq_rows,
    row_ids,
    sample_idx,
    fm_proj,
    ln_gain,
    w_up,
    w_down,
    w_lc,
    w_res,
    out_gain,
    cotangent,
    moment1,
    moment2,
):
    D = uniq_rows.shape[1]
    S = cotangent.shape[0]
    hid = w_up.shape[1]
    wide = w_down.shape[1]
    flat = w_up.shape[0]
    width = out_gain.shape[0]
    T = C * D
    vmem = pl.BlockSpec(memory_space=pltpu.VMEM)
    hbm = pl.BlockSpec(memory_space=pl.ANY)
    dma = pltpu.SemaphoreType.DMA
    layer_out, own, got, m1, m2 = pl.pallas_call(
        functools.partial(fused_kernel, C, D),
        out_shape=(
            pltpu.VMEM((S, 16 * width), BF16),
            pltpu.VMEM((D, width, T), F32),
            pltpu.VMEM((D, width, T), BF16),
            pltpu.VMEM((D, width, T), F32),
            pltpu.VMEM((D, T), F32),
        ),
        in_specs=[hbm] * 13,
        out_specs=(vmem,) * 5,
        scratch_shapes=[
            pltpu.VMEM((D, 8, C), jnp.int32),
            pltpu.VMEM((D, C * S), jnp.int32),
            pltpu.VMEM((8, T), BF16),
            pltpu.VMEM((1, flat), F32),
            pltpu.VMEM((8, T), BF16),
            pltpu.VMEM((16, T), BF16),
            pltpu.VMEM((1, width), F32),
            pltpu.VMEM((S, 16 * width), BF16),
            pltpu.VMEM((S, wide), BF16),
            pltpu.VMEM((C, D, S), jnp.int32),
            pltpu.VMEM((C, D, wide), BF16),
            pltpu.VMEM((C, D, S), jnp.int32),
            pltpu.VMEM((flat, hid), BF16),
            pltpu.VMEM((flat, hid), BF16),
            pltpu.VMEM((hid, wide), BF16),
            pltpu.VMEM((T, wide), F32),
            pltpu.VMEM((8 * T, width), BF16),
            pltpu.VMEM((512, 8 * T), BF16),
            pltpu.VMEM((C, 8 * D, 640), BF16),
            pltpu.VMEM((512, T), F32),
            pltpu.VMEM((640, width), BF16),
            pltpu.VMEM((128, T), F32),
            pltpu.VMEM((128, T), F32),
            pltpu.VMEM((T, 128), F32),
            pltpu.VMEM((2, S, flat), BF16),
            pltpu.VMEM((384, width), F32),
            pltpu.VMEM((2 * S, hid), F32),
            pltpu.VMEM((2 * S, wide), F32),
            pltpu.VMEM((3, 2 * S, wide // 3), BF16),
            pltpu.VMEM((3, 2 * S, wide // 3), BF16),
            pltpu.VMEM((2 * S, wide), F32),
            pltpu.VMEM((2, S, flat // 2), BF16),
            pltpu.VMEM((2, S, flat // 2), BF16),
            pltpu.VMEM((S, flat), F32),
            pltpu.VMEM((S, 16 * width), F32),
            pltpu.VMEM((2 * S, wide), F32),
            pltpu.VMEM((C, 8 * D, width), F32),
            pltpu.VMEM((C, 12 * D, T), BF16),
            pltpu.VMEM((C, 12 * D, T), BF16),
            pltpu.VMEM((2, D, T, T), BF16),
            pltpu.VMEM((D, width, T), BF16),
            dma((13,)),
            dma((C,)),
            dma((C,)),
            dma((C,)),
            dma((C,)),
            dma((6 * C,)),
            dma((6 * C,)),
            dma((13,)),
            dma((13,)),
        ],
        compiler_params=pltpu.CompilerParams(
            collective_id=0, has_side_effects=True, vmem_limit_bytes=36 * 1024 * 1024
        ),
        name="wukong_step",
    )(
        *(
            pltpu.with_memory_space_constraint(a, pltpu.HBM)
            for a in (
                uniq_rows,
                row_ids.transpose(1, 2, 0),
                sample_idx.T,
                fm_proj.T,
                ln_gain.reshape(1, flat),
                w_up,
                w_down,
                w_lc,
                w_res,
                out_gain.reshape(1, width),
                cotangent,
                moment1.transpose(0, 2, 1),
                moment2,
            )
        )
    )
    layer_out, own, got, m1, m2 = (
        pltpu.with_memory_space_constraint(a, pltpu.VMEM) for a in (layer_out, own, got, m1, m2)
    )
    layer_out, new_moment1, new_moment2, row_step = pl.pallas_call(
        functools.partial(moment_kernel, width),
        out_shape=(
            jax.ShapeDtypeStruct((S, 16 * width), BF16),
            jax.ShapeDtypeStruct((D, width, T), F32),
            jax.ShapeDtypeStruct((D, T), F32),
            jax.ShapeDtypeStruct((D, width, T), F32),
        ),
        in_specs=[vmem] * 5,
        out_specs=(hbm,) * 4,
        scratch_shapes=[
            pltpu.VMEM((D, width, T), F32),
            pltpu.VMEM((D, width, T), F32),
            pltpu.VMEM((D, T), F32),
            dma((2 + 2 * D,)),
        ],
        compiler_params=pltpu.CompilerParams(vmem_limit_bytes=8 * 1024 * 1024),
        name="moments",
    )(layer_out, own, got, m1, m2)
    return (
        layer_out,
        new_moment1.transpose(0, 2, 1),
        new_moment2,
        row_step.transpose(0, 2, 1),
    )


def step(C, R, *args):
    if args[0].shape[1] == 8 and C == 16 and R == 2:
        return fast_body(C, R, *args)
    return plain_body(*args)


def solution(mesh):
    return jax.shard_map(
        functools.partial(step, mesh.shape["col"], mesh.shape["row"]),
        mesh=mesh,
        in_specs=(
            P("row", "col", None),
            P("row", "col", None),
            P("row", "col"),
            P(),
            P(),
            P(None, "row"),
            P("row", None),
            P(),
            P(),
            P(),
            P(("row", "col"), None),
            P("col", "row", None),
            P("col", "row"),
        ),
        out_specs=(
            P(("row", "col"), None),
            P("col", "row", None),
            P("col", "row"),
            P("col", "row", None),
        ),
        check_vma=False,
    )
```

```python
import functools

import jax
import jax.numpy as jnp
from jax import lax
from jax.experimental import pallas as pl
from jax.experimental.pallas import tpu as pltpu
from jax.sharding import PartitionSpec as P

HIGH = lax.Precision.HIGHEST


def layer_norm(values, gain):
    centered = values - jnp.mean(values, -1, keepdims=True)
    inverse = lax.rsqrt(jnp.mean(centered * centered, -1, keepdims=True) + 1e-05)
    normed = centered * inverse
    return (normed * gain, normed, inverse)


def norm_back(grad_out, normed, inverse):
    first = jnp.mean(grad_out, -1, keepdims=True)
    second = jnp.mean(grad_out * normed, -1, keepdims=True)
    return (grad_out - first - normed * second) * inverse


def silu_grad(values):
    sigma = jax.nn.sigmoid(values)
    return sigma * (1.0 + values * (1.0 - sigma))


def plain_body(
    uniq_rows,
    row_ids,
    sample_idx,
    fm_proj,
    ln_gain,
    w_up,
    w_down,
    w_lc,
    w_res,
    out_gain,
    cotangent,
    moment1,
    moment2,
):
    columns = lax.axis_size("col")
    owners = lax.axis_size("row")
    slot_dev = uniq_rows.shape[1]
    width = out_gain.shape[0]
    uniq = uniq_rows.shape[2] // width
    samples = cotangent.shape[0]
    slots = slot_dev * columns
    vocab_dev = moment2.shape[1]
    rank = fm_proj.shape[1]
    fm_rows = w_down.shape[1] // width
    out_rows = w_res.shape[0]
    entry_iota = jnp.arange(uniq, dtype=jnp.int32)
    index_local = sample_idx.reshape(columns, samples, slot_dev)
    index = lax.all_to_all(index_local, "col", split_axis=0, concat_axis=2, tiled=True).reshape(
        samples, slots
    )
    picker = (index[:, :, None] == entry_iota).astype(jnp.bfloat16)
    moved = lax.all_to_all(uniq_rows, "col", split_axis=0, concat_axis=1, tiled=True)
    table = moved.reshape(slots, uniq, width)
    embed = jnp.einsum("stl,tle->ste", picker, table, preferred_element_type=jnp.float32).astype(
        jnp.bfloat16
    )
    compress = jnp.einsum("ste,tk->sek", embed, fm_proj, preferred_element_type=jnp.float32).astype(
        jnp.bfloat16
    )
    gram = jnp.einsum("ste,sek->stk", embed, compress, preferred_element_type=jnp.float32)
    flat = gram.reshape(samples, slots * rank)
    scaled, normed_in, inverse_in = layer_norm(flat, ln_gain)
    normal_in = scaled.astype(jnp.bfloat16)
    hidden_pre = jnp.dot(
        lax.all_gather(normal_in, "row", axis=0, tiled=True),
        w_up,
        preferred_element_type=jnp.float32,
    )
    hidden = jax.nn.silu(hidden_pre).astype(jnp.bfloat16)
    part_rows = hidden
    fm_out = lax.psum_scatter(
        jnp.dot(part_rows, w_down, preferred_element_type=jnp.float32),
        "row",
        scatter_dimension=0,
        tiled=True,
    )
    linear = jnp.einsum("lt,ste->sle", w_lc, embed, preferred_element_type=jnp.float32)
    joined = jnp.concatenate([fm_out.reshape(samples, fm_rows, width), linear], 1)
    normed_out, normed_rows, inverse_rows = layer_norm(joined, out_gain)
    residual = jnp.einsum("ot,ste->soe", w_res, embed, preferred_element_type=jnp.float32)
    layer_out = (normed_out + residual).reshape(samples, out_rows * width).astype(jnp.bfloat16)
    upstream = cotangent.astype(jnp.float32).reshape(samples, out_rows, width)
    grad_joined = norm_back(upstream * out_gain, normed_rows, inverse_rows)
    grad_fm = grad_joined[:, :fm_rows].reshape(samples, fm_rows * width).astype(jnp.bfloat16)
    grad_hidden = lax.dot_general(
        lax.all_gather(grad_fm, "row", axis=0, tiled=True),
        w_down,
        (((1,), (1,)), ((), ())),
        preferred_element_type=jnp.float32,
    )
    grad_pre = (grad_hidden * silu_grad(hidden_pre)).astype(jnp.bfloat16)
    part_rows = grad_pre
    grad_flat = lax.psum_scatter(
        lax.dot_general(
            part_rows, w_up, (((1,), (1,)), ((), ())), preferred_element_type=jnp.float32
        ).astype(jnp.bfloat16),
        "row",
        scatter_dimension=0,
        tiled=True,
    ).astype(jnp.float32)
    grad_gram = norm_back(grad_flat * ln_gain, normed_in, inverse_in).reshape(samples, slots, rank)
    grad_embed = jnp.einsum("stk,sek->ste", grad_gram, compress.astype(jnp.float32), precision=HIGH)
    grad_comp = jnp.einsum(
        "ste,stk->sek", embed, grad_gram, precision=HIGH, preferred_element_type=jnp.float32
    )
    grad_embed = grad_embed + jnp.einsum(
        "tk,sek->ste", fm_proj.astype(jnp.float32), grad_comp, precision=HIGH
    )
    grad_embed = grad_embed + jnp.einsum(
        "lt,sle->ste", w_lc.astype(jnp.float32), grad_joined[:, fm_rows:], precision=HIGH
    )
    grad_embed = grad_embed + jnp.einsum(
        "ot,soe->ste", w_res.astype(jnp.float32), upstream, precision=HIGH
    )
    list_grads = jnp.einsum("stl,ste->tle", picker.astype(jnp.float32), grad_embed, precision=HIGH)
    returned = lax.all_to_all(
        list_grads.reshape(columns, slot_dev, uniq * width),
        "col",
        split_axis=0,
        concat_axis=0,
        tiled=True,
    )
    entry_grads = returned.reshape(columns * slot_dev * uniq, width)
    row_list = row_ids.reshape(-1)
    slot_of = jnp.broadcast_to(
        jnp.arange(slot_dev, dtype=jnp.int32)[None, :, None], row_ids.shape
    ).reshape(-1)
    owner = row_list // vocab_dev
    target = slot_of * vocab_dev + row_list % vocab_dev
    span = slot_dev * vocab_dev
    entries = row_list.shape[0]
    capacity = 5 * entries // (4 * owners)
    onehot = (owner[:, None] == jnp.arange(owners, dtype=jnp.int32)).astype(jnp.int32)
    before = jnp.cumsum(onehot, 0) - onehot
    place = jnp.sum(before * onehot, 1)
    target_slot = owner * capacity + place
    bucket = jnp.zeros((owners * capacity, width), jnp.float32).at[target_slot].set(entry_grads)
    labels = (
        jnp.full((owners * capacity,), -1.0, jnp.float32)
        .at[target_slot]
        .set(target.astype(jnp.float32))
    )
    got_rows, got_labels = (
        lax.all_to_all(
            bucket.reshape(owners, capacity, width), "row", split_axis=0, concat_axis=0, tiled=True
        ),
        lax.all_to_all(
            labels.reshape(owners, capacity), "row", split_axis=0, concat_axis=0, tiled=True
        ),
    )
    segment = jnp.where(got_labels >= 0.0, got_labels, float(span)).astype(jnp.int32).reshape(-1)
    summed = jax.ops.segment_sum(got_rows.reshape(-1, width), segment, num_segments=span + 1)[:span]
    row_grads = summed.reshape(slot_dev, vocab_dev, width)
    new_moment1 = 0.9 * moment1 + 0.1 * row_grads
    new_moment2 = 0.99 * moment2 + 0.01 * jnp.mean(row_grads * row_grads, -1)
    row_step = new_moment1 * lax.rsqrt(new_moment2)[..., None]
    return (layer_out, new_moment1, new_moment2, row_step)


F32 = jnp.float32
BF16 = jnp.bfloat16
NT = (((1,), (1,)), ((), ()))


def iota(shape, dim):
    return lax.broadcasted_iota(jnp.int32, shape, dim)


def matmul(a, b, dims=(((1,), (0,)), ((), ())), precision=None):
    return lax.dot_general(a, b, dims, precision=precision, preferred_element_type=F32)


def fused_kernel(
    C,
    D,
    uniq,
    rid_in,
    sidx_in,
    fmp_in,
    gain_in,
    wup,
    wdn,
    wlc_in,
    wres_in,
    og_in,
    cot_in,
    m1_in,
    m2_in,
    lay_out,
    rg_out,
    pr,
    m1_out,
    m2_out,
    rid,
    fmp,
    gain,
    wlc,
    wres,
    og,
    cot,
    cpeer,
    land,
    iland,
    wraw,
    wp,
    wd,
    t32,
    tst,
    lm,
    lmask,
    arep,
    rmat,
    nrm,
    ggr,
    idxn,
    nall,
    y,
    ds,
    c32,
    fsend,
    frecv,
    fm,
    qsend,
    qrecv,
    gq,
    lay32,
    gf32,
    lge,
    sb,
    rland,
    oh,
    ps,
    loc,
    sa,
    ra,
    sx,
    rx,
):
    S, E, U, K, T = 16, 192, 8, 8, 128
    FC, QC, PACE = 2, 2, 0
    me = lax.axis_index("col")
    mr = lax.axis_index("row")
    other = 1 - mr

    def to_col(i):
        return lax.rem(me + i, C)

    def rcopy(src, dst, ssem, rsem, where):
        return pltpu.make_async_remote_copy(
            src_ref=src,
            dst_ref=dst,
            send_sem=ssem,
            recv_sem=rsem,
            device_id=where,
            device_id_type=pl.DeviceIdType.MESH,
        )

    def row_send(src, dst, sem):
        copy = rcopy(src, dst, sx.at[sem], rx.at[sem], {"row": other})
        copy.start()
        return copy

    barrier = pltpu.get_barrier_semaphore()
    for i in range(1, C):
        pl.semaphore_signal(
            barrier, inc=1, device_id={"col": to_col(i)}, device_id_type=pl.DeviceIdType.MESH
        )
    pl.semaphore_signal(
        barrier, inc=1, device_id={"row": other}, device_id_type=pl.DeviceIdType.MESH
    )
    tile = lambda p: sidx_in.at[:, pl.ds(pl.multiple_of(p * S // T * T, T), T)]
    own_idx = pltpu.make_async_copy(tile(me), iland.at[me], loc.at[0])
    own_idx.start()
    cp_up = pltpu.make_async_copy(wup, wraw, loc.at[1])
    cp_dn = pltpu.make_async_copy(wdn, wd, loc.at[2])
    own_rows = pltpu.make_async_copy(uniq.at[me], land.at[me], loc.at[3])
    own_rows.start()
    small = [
        pltpu.make_async_copy(a, b, loc.at[4 + n])
        for n, (a, b) in enumerate(
            (
                (rid_in, rid),
                (fmp_in, fmp),
                (gain_in, gain),
                (wlc_in, wlc),
                (wres_in, wres),
                (og_in, og),
                (cot_in, cot),
                (m2_in, m2_out),
            )
        )
    ]
    for cp in small:
        cp.start()
    cp_m1 = pltpu.make_async_copy(m1_in, m1_out, loc.at[12])
    cp_up.start()
    cp_dn.start()
    cp_m1.start()
    pl.semaphore_wait(barrier, C)

    order = sorted(range(1, C), key=lambda i: -min(i, C - i))
    for i in order:
        p = to_col(i)
        rcopy(tile(p), iland.at[me], sa.at[0], ra.at[0], {"col": p}).start()
    for i in order:
        p = to_col(i)
        rcopy(uniq.at[p], land.at[me], sa.at[1], ra.at[1], {"col": p}).start()
    most = pl.ds(0, C - 1)
    all_idx = rcopy(iland.at[most], iland.at[most], sa.at[0], ra.at[0], {"row": other})
    all_rows = rcopy(land.at[most], land.at[most], sa.at[1], ra.at[1], {"row": other})
    c_copy = row_send(cot_in.at[:, pl.ds(0, 8 * E)], cpeer, 0)

    to, at = iota((256, 256), 0), iota((256, 256), 1)
    perm = (((to & 31) * 8 + (to >> 5)) == at).astype(F32).astype(BF16)
    for cp in small:
        cp.wait()
    cp_up.wait()
    for g in range(4):
        blk = matmul(perm, wraw[g * 256 : (g + 1) * 256, :]).astype(BF16)
        for k in range(K):
            wp[k * T + g * 32 : k * T + (g + 1) * 32, :] = blk[k * 32 : (k + 1) * 32, :]
    lane = iota((K, K * T), 1)
    spread = jnp.where((lane & 7) == iota((K, K * T), 0), gain[...], 0.0)
    fold = ((iota((K * T, T), 0) >> 3) == iota((K * T, T), 1)).astype(F32)
    gk = matmul(spread, fold, precision=HIGH)

    amat = jnp.concatenate(
        [
            fmp[...].astype(F32),
            wlc[...].astype(F32),
            wres[...].astype(F32),
        ],
        0,
    )
    for j in range(32):
        arep[j * S : (j + 1) * S, :] = jnp.broadcast_to(amat[j : j + 1, :], (S, T))

    place = (iota((C, T), 0) == (iota((C, T), 1) >> 3)).astype(F32)
    wide = matmul(rid[...].astype(F32).reshape(D * U, C), place, precision=HIGH).reshape(D, U, T)
    mine = iota((D, U, T), 1) == (iota((D, U, T), 2) & (U - 1))
    labels = jnp.sum(jnp.where(mine, wide, 0.0), 1).astype(jnp.int32)
    target = iota((T, T), 0)
    for i in range(2):
        local = labels - (mr if i == 0 else other) * T
        for d in range(D):
            oh[i, d] = jnp.where(
                target == jnp.broadcast_to(local[d : d + 1, :], (T, T)), 1.0, 0.0
            ).astype(BF16)

    own_idx.wait()
    all_idx.wait_recv()
    ix = iland[...].astype(F32).reshape(T, T)
    mine = lax.rem(me, T // S) * S
    tiled = (iota((T, T), 0) == (iota((T, T), 1) & (S - 1)) + mine).astype(F32)
    idx_n = matmul(ix, tiled, precision=HIGH)
    idxn[...] = idx_n
    idx_t = idx_n.T
    for u in range(U):
        for q in range(4):
            lm[q * T : (q + 1) * T, u * T : (u + 1) * T] = jnp.where(
                idx_t == float(u), arep[q * T : (q + 1) * T, :], 0.0
            ).astype(BF16)
    entry = iota((U, T), 0).astype(F32)

    def fill(src, at, slots=range(0, T, 2)):
        for t in slots:
            rows = [
                jnp.where(
                    jnp.broadcast_to(idxn[v : v + 1, :], (U, T)) == entry,
                    jnp.broadcast_to(src[v : v + 1, :], (U, T)),
                    0.0,
                )
                for v in (t, t + 1)
            ]
            lmask[t // D, t % D * U : (t % D + 2) * U, at * T : (at + 1) * T] = jnp.concatenate(
                rows, 0
            ).astype(BF16)

    for q in range(4):
        ggr[...] = arep[q * T : (q + 1) * T, :].T
        fill(ggr, (q + 3) & 3)
    upstream = cot[...].astype(F32)
    for o in range(16):
        rmat[(8 + o) * S : (9 + o) * S, :] = upstream[:, o * E : (o + 1) * E].astype(BF16)

    own_rows.wait()
    all_rows.wait_recv()
    t32[...] = land[...].astype(F32).reshape(T, U * E)
    for u in range(U):
        tst[u * T : (u + 1) * T, :] = t32[:, u * E : (u + 1) * E].astype(BF16)

    comp = matmul(lm[0:T, :], tst[...]).astype(BF16)
    rmat[512:640, :] = comp
    z = matmul(comp, tst[...], NT)
    gram = jnp.where(idx_t == 0.0, z[:, 0:T], 0.0)
    for u in range(1, U):
        gram = gram + jnp.where(idx_t == float(u), z[:, u * T : (u + 1) * T], 0.0)
    n_flat = float(K * T)
    g3 = gram.reshape(K, S, T)
    mu = jnp.sum(jnp.sum(g3, 0), -1, keepdims=True) / n_flat
    cent = g3 - mu[None]
    inv_in = lax.rsqrt(jnp.sum(jnp.sum(cent * cent, 0), -1, keepdims=True) / n_flat + 1e-05)
    normed_in = cent * inv_in[None]
    nrm[...] = normed_in.reshape(K * S, T)
    for k in range(K):
        nall[0, :, k * T : (k + 1) * T] = (normed_in[k] * gk[k : k + 1, :]).astype(BF16)
    n_copy = row_send(nall.at[0], nall.at[1], 1)

    y[...] = matmul(lm[T:512, :], tst[...])
    gain_out = og[...]
    c_copy.wait_recv()
    c32[0:S, :] = upstream[:, 0 : 8 * E]
    c32[S : 2 * S, :] = cpeer[...].astype(F32)
    up_fm = jnp.concatenate([c32[:, o * E : (o + 1) * E] for o in range(8)], 0) * gain_out
    up_mean = jnp.mean(up_fm, -1, keepdims=True)
    cp_dn.wait()
    n_copy.wait_recv()
    hp = matmul(nall[...].reshape(2 * S, K * T), wp[...])
    sg = jax.nn.sigmoid(hp)
    hid = (hp * sg).astype(BF16)
    f_copies = []
    for c in range(FC):
        cols = slice(c * 8 * E // FC, (c + 1) * 8 * E // FC)
        fp = matmul(hid, wd[:, cols])
        fm[:, cols] = fp
        fsend[c, 0:S] = fp[S : 2 * S].astype(BF16)
        fsend[c, S : 2 * S] = fp[0:S].astype(BF16)
        f_copies.append(row_send(fsend.at[c], frecv.at[c], 2 + c))
    ds[...] = sg * (1.0 + hp * (1.0 - sg))

    def out_norm(joined, o):
        up = upstream[:, o * E : (o + 1) * E]
        c = joined - jnp.mean(joined, -1, keepdims=True)
        inv = lax.rsqrt(jnp.mean(c * c, -1, keepdims=True) + 1e-05)
        nr = c * inv
        return nr, norm_back(up * gain_out, nr, inv)

    for o in range(8, 16):
        nr, gj = out_norm(y[(o - 8) * S : (o - 7) * S, :], o)
        lay32[:, o * E : (o + 1) * E] = nr * gain_out + y[(8 + o) * S : (9 + o) * S, :]
        rmat[(o - 8) * S : (o - 7) * S, :] = gj.astype(BF16)

    normed_fm, gh = [], None
    per = 8 // FC
    for c in range(FC):
        f_copies[c].wait_recv()
        cols = slice(c * per * E, (c + 1) * per * E)
        rows = slice(c * per * 2 * S, (c + 1) * per * 2 * S)
        fm[:, cols] += frecv[c].astype(F32)
        joined = jnp.concatenate(
            [fm[:, o * E : (o + 1) * E] for o in range(c * per, (c + 1) * per)], 0
        )
        cen = joined - jnp.mean(joined, -1, keepdims=True)
        inv_fm = lax.rsqrt(jnp.mean(cen * cen, -1, keepdims=True) + 1e-05)
        normed = cen * inv_fm
        across = jnp.mean(up_fm[rows] * cen, -1, keepdims=True) * inv_fm
        grad_fm = (up_fm[rows] - up_mean[rows] - normed * across) * inv_fm
        for o in range(per):
            at = (c * per + o) * E
            gf32[:, at : at + E] = grad_fm[o * 2 * S : (o + 1) * 2 * S]
            normed_fm.append(normed[o * 2 * S : o * 2 * S + S])
        part = matmul(gf32[:, cols].astype(BF16), wd[:, cols], NT)
        gh = part if gh is None else gh + part
    gp = (gh * ds[...]).astype(BF16)
    q_copies = []
    for c in range(QC):
        cols = slice(c * K * T // QC, (c + 1) * K * T // QC)
        part = matmul(gp, wp[cols, :], NT)
        gq[:, cols] = part[0:S]
        qsend[c] = part[S : 2 * S].astype(BF16)
        q_copies.append(row_send(qsend.at[c], qrecv.at[c], 2 + FC + c))
    for o in range(8):
        lay32[:, o * E : (o + 1) * E] = (
            normed_fm[o] * gain_out + y[(8 + o) * S : (9 + o) * S, :]
        )
    lay_out[...] = lay32[...].astype(BF16)
    lge[...] = matmul(
        lmask[:, :, 0:384].reshape(C * D * U, 384), rmat[0:384, :]
    ).reshape(C, D * U, E)
    for c in range(QC):
        q_copies[c].wait_recv()
    width = K // QC
    qs = [
        (
            gq[:, k * T : (k + 1) * T]
            + qrecv[k // width, :, k % width * T : (k % width + 1) * T].astype(F32)
        )
        * gk[k : k + 1, :]
        for k in range(K)
    ]
    ns = [nrm[k * S : (k + 1) * S, :] for k in range(K)]
    first = jnp.sum(sum(qs), -1, keepdims=True) / n_flat
    second = jnp.sum(sum(q * n for q, n in zip(qs, ns)), -1, keepdims=True) / n_flat
    for k in range(K):
        ggr[k * S : (k + 1) * S, :] = (qs[k] - first - ns[k] * second) * inv_in
    gg = ggr[...]
    for u in range(U):
        lm[0:T, u * T : (u + 1) * T] = jnp.where(idx_t == float(u), gg, 0.0).astype(BF16)
    ggr[...] = gg.T
    rmat[384:512, :] = matmul(lm[0:T, :], tst[...]).astype(BF16)

    units = []
    for half in range(2):
        at = half * 32
        fill(ggr, 4, [t for t in range(0, T, 2) if t % D // 4 == half])
        part = matmul(lmask[:, at : at + 32, 384:640].reshape(C * 32, 256), rmat[384:640, :])
        part = part.reshape(C, 32, E) + lge[:, at : at + 32, :]
        row = half * 48
        top = part[:, :, T:E]
        sb[:, row : row + 16, :] = jnp.concatenate([top[:, :16], top[:, 16:]], -1).astype(BF16)
        sb[:, row + 16 : row + 48, :] = part[:, :, 0:T].astype(BF16)
        for j in range(half * 3, half * 3 + 3):
            if PACE and j >= PACE:
                units[j - PACE].wait_send()
            cut = pl.ds(j * 16, 16)
            for i in order:
                p = to_col(i)
                rcopy(
                    sb.at[p, cut], rland.at[me, cut], sa.at[2 + j], ra.at[2 + j], {"col": p}
                ).start()
            units.append(
                rcopy(
                    sb.at[most, cut], rland.at[most, cut], sa.at[2 + j], ra.at[2 + j], {"row": other}
                )
            )
    rland[me] = sb[me]

    p_copies = []
    for j in range(6):
        units[j].wait_recv()
        base, kind = j // 3 * 4, j % 3
        both = rland[:, j * 16 : (j + 1) * 16, :].astype(F32)
        pieces = []
        for h in range(2):
            x = both[:, h * U : (h + 1) * U, :].reshape(T, T).T.astype(BF16)
            if kind == 0:
                pieces.append((base + h, T, E, x[: E - T]))
                pieces.append((base + 2 + h, T, E, x[E - T :]))
            else:
                pieces.append((base + 2 * (kind - 1) + h, 0, T, x))
        for d, a, b, x in pieces:
            ps[d, a:b, :] = matmul(x, oh[1, d], NT).astype(BF16)
        if kind == 0:
            part = (pl.ds(base, 4), pl.ds(T, E - T))
        else:
            part = (pl.ds(base + 2 * (kind - 1), 2), pl.ds(0, T))
        p_copies.append(row_send(ps.at[part], pr.at[part], 2 + FC + QC + j))
        for d, a, b, x in pieces:
            rg_out[d, a:b, :] = matmul(x, oh[0, d], NT)
    cp_m1.wait()
    for cp in p_copies:
        cp.wait_recv()
    for cp in (
        all_idx,
        all_rows,
        c_copy,
        n_copy,
        *f_copies,
        *q_copies,
        *(units[6 - PACE :] if PACE else units),
        *p_copies,
    ):
        cp.wait_send()


def moment_kernel(
    width, lay, own, got, m1, m2, lay_out, m1_out, m2_out, step_out, mv, sv, m2v, sem
):
    D = own.shape[0]
    copies = [pltpu.make_async_copy(lay, lay_out, sem.at[0])]
    copies[0].start()
    for d in range(D):
        g = own[d] + got[d].astype(F32)
        first = 0.9 * m1[d] + 0.1 * g
        second = 0.99 * m2[d : d + 1, :] + 0.01 * (jnp.sum(g * g, 0, keepdims=True) / width)
        mv[d] = first
        m2v[d : d + 1, :] = second
        sv[d] = first * lax.rsqrt(second)
        for n, (a, b) in enumerate(((mv, m1_out), (sv, step_out))):
            copies.append(pltpu.make_async_copy(a.at[d], b.at[d], sem.at[2 + 2 * d + n]))
            copies[-1].start()
    copies.append(pltpu.make_async_copy(m2v, m2_out, sem.at[1]))
    copies[-1].start()
    for cp in copies:
        cp.wait()


def fast_body(
    C,
    R,
    uniq_rows,
    row_ids,
    sample_idx,
    fm_proj,
    ln_gain,
    w_up,
    w_down,
    w_lc,
    w_res,
    out_gain,
    cotangent,
    moment1,
    moment2,
):
    D = uniq_rows.shape[1]
    S = cotangent.shape[0]
    hid = w_up.shape[1]
    wide = w_down.shape[1]
    flat = w_up.shape[0]
    width = out_gain.shape[0]
    T = C * D
    vmem = pl.BlockSpec(memory_space=pltpu.VMEM)
    hbm = pl.BlockSpec(memory_space=pl.ANY)
    dma = pltpu.SemaphoreType.DMA
    layer_out, own, got, m1, m2 = pl.pallas_call(
        functools.partial(fused_kernel, C, D),
        out_shape=(
            pltpu.VMEM((S, 16 * width), BF16),
            pltpu.VMEM((D, width, T), F32),
            pltpu.VMEM((D, width, T), BF16),
            pltpu.VMEM((D, width, T), F32),
            pltpu.VMEM((D, T), F32),
        ),
        in_specs=[hbm] * 13,
        out_specs=(vmem,) * 5,
        scratch_shapes=[
            pltpu.VMEM((D, 8, C), jnp.int32),
            pltpu.VMEM((8, T), BF16),
            pltpu.VMEM((1, flat), F32),
            pltpu.VMEM((8, T), BF16),
            pltpu.VMEM((16, T), BF16),
            pltpu.VMEM((1, width), F32),
            pltpu.VMEM((S, 16 * width), BF16),
            pltpu.VMEM((S, wide), BF16),
            pltpu.VMEM((C, D, wide), BF16),
            pltpu.VMEM((C, D, T), jnp.int32),
            pltpu.VMEM((flat, hid), BF16),
            pltpu.VMEM((flat, hid), BF16),
            pltpu.VMEM((hid, wide), BF16),
            pltpu.VMEM((T, wide), F32),
            pltpu.VMEM((8 * T, width), BF16),
            pltpu.VMEM((512, 8 * T), BF16),
            pltpu.VMEM((C, 8 * D, 640), BF16),
            pltpu.VMEM((512, T), F32),
            pltpu.VMEM((640, width), BF16),
            pltpu.VMEM((128, T), F32),
            pltpu.VMEM((128, T), F32),
            pltpu.VMEM((T, 128), F32),
            pltpu.VMEM((2, S, flat), BF16),
            pltpu.VMEM((384, width), F32),
            pltpu.VMEM((2 * S, hid), F32),
            pltpu.VMEM((2 * S, wide), F32),
            pltpu.VMEM((2, 2 * S, wide // 2), BF16),
            pltpu.VMEM((2, 2 * S, wide // 2), BF16),
            pltpu.VMEM((2 * S, wide), F32),
            pltpu.VMEM((2, S, flat // 2), BF16),
            pltpu.VMEM((2, S, flat // 2), BF16),
            pltpu.VMEM((S, flat), F32),
            pltpu.VMEM((S, 16 * width), F32),
            pltpu.VMEM((2 * S, wide), F32),
            pltpu.VMEM((C, 8 * D, width), F32),
            pltpu.VMEM((C, 12 * D, T), BF16),
            pltpu.VMEM((C, 12 * D, T), BF16),
            pltpu.VMEM((2, D, T, T), BF16),
            pltpu.VMEM((D, width, T), BF16),
            dma((13,)),
            dma((8,)),
            dma((8,)),
            dma((13,)),
            dma((13,)),
        ],
        compiler_params=pltpu.CompilerParams(
            collective_id=0, has_side_effects=True, vmem_limit_bytes=36 * 1024 * 1024
        ),
        name="wukong_step",
    )(
        *(
            pltpu.with_memory_space_constraint(a, pltpu.HBM)
            for a in (
                uniq_rows,
                row_ids.transpose(1, 2, 0),
                sample_idx.T,
                fm_proj.T,
                ln_gain.reshape(1, flat),
                w_up,
                w_down,
                w_lc,
                w_res,
                out_gain.reshape(1, width),
                cotangent,
                moment1.transpose(0, 2, 1),
                moment2,
            )
        )
    )
    layer_out, own, got, m1, m2 = (
        pltpu.with_memory_space_constraint(a, pltpu.VMEM) for a in (layer_out, own, got, m1, m2)
    )
    layer_out, new_moment1, new_moment2, row_step = pl.pallas_call(
        functools.partial(moment_kernel, width),
        out_shape=(
            jax.ShapeDtypeStruct((S, 16 * width), BF16),
            jax.ShapeDtypeStruct((D, width, T), F32),
            jax.ShapeDtypeStruct((D, T), F32),
            jax.ShapeDtypeStruct((D, width, T), F32),
        ),
        in_specs=[vmem] * 5,
        out_specs=(hbm,) * 4,
        scratch_shapes=[
            pltpu.VMEM((D, width, T), F32),
            pltpu.VMEM((D, width, T), F32),
            pltpu.VMEM((D, T), F32),
            dma((2 + 2 * D,)),
        ],
        compiler_params=pltpu.CompilerParams(vmem_limit_bytes=8 * 1024 * 1024),
        name="moments",
    )(layer_out, own, got, m1, m2)
    return (
        layer_out,
        new_moment1.transpose(0, 2, 1),
        new_moment2,
        row_step.transpose(0, 2, 1),
    )


def step(C, R, *args):
    if args[0].shape[1] == 8 and C == 16 and R == 2:
        return fast_body(C, R, *args)
    return plain_body(*args)


def solution(mesh):
    return jax.shard_map(
        functools.partial(step, mesh.shape["col"], mesh.shape["row"]),
        mesh=mesh,
        in_specs=(
            P("row", "col", None),
            P("row", "col", None),
            P("row", "col"),
            P(),
            P(),
            P(None, "row"),
            P("row", None),
            P(),
            P(),
            P(),
            P(("row", "col"), None),
            P("col", "row", None),
            P("col", "row"),
        ),
        out_specs=(
            P(("row", "col"), None),
            P("col", "row", None),
            P("col", "row"),
            P("col", "row", None),
        ),
        check_vma=False,
    )
```

```python
import functools

import jax
import jax.numpy as jnp
from jax import lax
from jax.experimental import pallas as pl
from jax.experimental.pallas import tpu as pltpu
from jax.sharding import PartitionSpec as P

HIGH = lax.Precision.HIGHEST


def layer_norm(values, gain):
    centered = values - jnp.mean(values, -1, keepdims=True)
    inverse = lax.rsqrt(jnp.mean(centered * centered, -1, keepdims=True) + 1e-05)
    normed = centered * inverse
    return (normed * gain, normed, inverse)


def norm_back(grad_out, normed, inverse):
    first = jnp.mean(grad_out, -1, keepdims=True)
    second = jnp.mean(grad_out * normed, -1, keepdims=True)
    return (grad_out - first - normed * second) * inverse


def silu_grad(values):
    sigma = jax.nn.sigmoid(values)
    return sigma * (1.0 + values * (1.0 - sigma))


def plain_body(
    uniq_rows,
    row_ids,
    sample_idx,
    fm_proj,
    ln_gain,
    w_up,
    w_down,
    w_lc,
    w_res,
    out_gain,
    cotangent,
    moment1,
    moment2,
):
    columns = lax.axis_size("col")
    owners = lax.axis_size("row")
    slot_dev = uniq_rows.shape[1]
    width = out_gain.shape[0]
    uniq = uniq_rows.shape[2] // width
    samples = cotangent.shape[0]
    slots = slot_dev * columns
    vocab_dev = moment2.shape[1]
    rank = fm_proj.shape[1]
    fm_rows = w_down.shape[1] // width
    out_rows = w_res.shape[0]
    entry_iota = jnp.arange(uniq, dtype=jnp.int32)
    index_local = sample_idx.reshape(columns, samples, slot_dev)
    index = lax.all_to_all(index_local, "col", split_axis=0, concat_axis=2, tiled=True).reshape(
        samples, slots
    )
    picker = (index[:, :, None] == entry_iota).astype(jnp.bfloat16)
    moved = lax.all_to_all(uniq_rows, "col", split_axis=0, concat_axis=1, tiled=True)
    table = moved.reshape(slots, uniq, width)
    embed = jnp.einsum("stl,tle->ste", picker, table, preferred_element_type=jnp.float32).astype(
        jnp.bfloat16
    )
    compress = jnp.einsum("ste,tk->sek", embed, fm_proj, preferred_element_type=jnp.float32).astype(
        jnp.bfloat16
    )
    gram = jnp.einsum("ste,sek->stk", embed, compress, preferred_element_type=jnp.float32)
    flat = gram.reshape(samples, slots * rank)
    scaled, normed_in, inverse_in = layer_norm(flat, ln_gain)
    normal_in = scaled.astype(jnp.bfloat16)
    hidden_pre = jnp.dot(
        lax.all_gather(normal_in, "row", axis=0, tiled=True),
        w_up,
        preferred_element_type=jnp.float32,
    )
    hidden = jax.nn.silu(hidden_pre).astype(jnp.bfloat16)
    part_rows = hidden
    fm_out = lax.psum_scatter(
        jnp.dot(part_rows, w_down, preferred_element_type=jnp.float32),
        "row",
        scatter_dimension=0,
        tiled=True,
    )
    linear = jnp.einsum("lt,ste->sle", w_lc, embed, preferred_element_type=jnp.float32)
    joined = jnp.concatenate([fm_out.reshape(samples, fm_rows, width), linear], 1)
    normed_out, normed_rows, inverse_rows = layer_norm(joined, out_gain)
    residual = jnp.einsum("ot,ste->soe", w_res, embed, preferred_element_type=jnp.float32)
    layer_out = (normed_out + residual).reshape(samples, out_rows * width).astype(jnp.bfloat16)
    upstream = cotangent.astype(jnp.float32).reshape(samples, out_rows, width)
    grad_joined = norm_back(upstream * out_gain, normed_rows, inverse_rows)
    grad_fm = grad_joined[:, :fm_rows].reshape(samples, fm_rows * width).astype(jnp.bfloat16)
    grad_hidden = lax.dot_general(
        lax.all_gather(grad_fm, "row", axis=0, tiled=True),
        w_down,
        (((1,), (1,)), ((), ())),
        preferred_element_type=jnp.float32,
    )
    grad_pre = (grad_hidden * silu_grad(hidden_pre)).astype(jnp.bfloat16)
    part_rows = grad_pre
    grad_flat = lax.psum_scatter(
        lax.dot_general(
            part_rows, w_up, (((1,), (1,)), ((), ())), preferred_element_type=jnp.float32
        ).astype(jnp.bfloat16),
        "row",
        scatter_dimension=0,
        tiled=True,
    ).astype(jnp.float32)
    grad_gram = norm_back(grad_flat * ln_gain, normed_in, inverse_in).reshape(samples, slots, rank)
    grad_embed = jnp.einsum("stk,sek->ste", grad_gram, compress.astype(jnp.float32), precision=HIGH)
    grad_comp = jnp.einsum(
        "ste,stk->sek", embed, grad_gram, precision=HIGH, preferred_element_type=jnp.float32
    )
    grad_embed = grad_embed + jnp.einsum(
        "tk,sek->ste", fm_proj.astype(jnp.float32), grad_comp, precision=HIGH
    )
    grad_embed = grad_embed + jnp.einsum(
        "lt,sle->ste", w_lc.astype(jnp.float32), grad_joined[:, fm_rows:], precision=HIGH
    )
    grad_embed = grad_embed + jnp.einsum(
        "ot,soe->ste", w_res.astype(jnp.float32), upstream, precision=HIGH
    )
    list_grads = jnp.einsum("stl,ste->tle", picker.astype(jnp.float32), grad_embed, precision=HIGH)
    returned = lax.all_to_all(
        list_grads.reshape(columns, slot_dev, uniq * width),
        "col",
        split_axis=0,
        concat_axis=0,
        tiled=True,
    )
    entry_grads = returned.reshape(columns * slot_dev * uniq, width)
    row_list = row_ids.reshape(-1)
    slot_of = jnp.broadcast_to(
        jnp.arange(slot_dev, dtype=jnp.int32)[None, :, None], row_ids.shape
    ).reshape(-1)
    owner = row_list // vocab_dev
    target = slot_of * vocab_dev + row_list % vocab_dev
    span = slot_dev * vocab_dev
    entries = row_list.shape[0]
    capacity = 5 * entries // (4 * owners)
    onehot = (owner[:, None] == jnp.arange(owners, dtype=jnp.int32)).astype(jnp.int32)
    before = jnp.cumsum(onehot, 0) - onehot
    place = jnp.sum(before * onehot, 1)
    target_slot = owner * capacity + place
    bucket = jnp.zeros((owners * capacity, width), jnp.float32).at[target_slot].set(entry_grads)
    labels = (
        jnp.full((owners * capacity,), -1.0, jnp.float32)
        .at[target_slot]
        .set(target.astype(jnp.float32))
    )
    got_rows, got_labels = (
        lax.all_to_all(
            bucket.reshape(owners, capacity, width), "row", split_axis=0, concat_axis=0, tiled=True
        ),
        lax.all_to_all(
            labels.reshape(owners, capacity), "row", split_axis=0, concat_axis=0, tiled=True
        ),
    )
    segment = jnp.where(got_labels >= 0.0, got_labels, float(span)).astype(jnp.int32).reshape(-1)
    summed = jax.ops.segment_sum(got_rows.reshape(-1, width), segment, num_segments=span + 1)[:span]
    row_grads = summed.reshape(slot_dev, vocab_dev, width)
    new_moment1 = 0.9 * moment1 + 0.1 * row_grads
    new_moment2 = 0.99 * moment2 + 0.01 * jnp.mean(row_grads * row_grads, -1)
    row_step = new_moment1 * lax.rsqrt(new_moment2)[..., None]
    return (layer_out, new_moment1, new_moment2, row_step)


F32 = jnp.float32
BF16 = jnp.bfloat16
NT = (((1,), (1,)), ((), ()))


def iota(shape, dim):
    return lax.broadcasted_iota(jnp.int32, shape, dim)


def matmul(a, b, dims=(((1,), (0,)), ((), ())), precision=None):
    return lax.dot_general(a, b, dims, precision=precision, preferred_element_type=F32)


def fused_kernel(
    C,
    D,
    uniq,
    rid_in,
    sidx_in,
    fmp_in,
    gain_in,
    wup,
    wdn,
    wlc_in,
    wres_in,
    og_in,
    cot_in,
    m1_in,
    m2_in,
    lay_out,
    rg_out,
    pr,
    m1_out,
    m2_out,
    rid,
    fmp,
    gain,
    wlc,
    wres,
    og,
    cot,
    cpeer,
    land,
    iland,
    wraw,
    wp,
    wd,
    t32,
    tst,
    lm,
    lmask,
    arep,
    rmat,
    nrm,
    ggr,
    idxn,
    nall,
    y,
    ds,
    c32,
    fsend,
    frecv,
    fm,
    qsend,
    qrecv,
    gq,
    lay32,
    gf32,
    lge,
    sb,
    rland,
    oh,
    ps,
    ridp,
    yb,
    rlandp,
    ohp,
    loc,
    sa,
    ra,
    sx,
    rx,
):
    S, E, U, K, T = 16, 192, 8, 8, 128
    FC, QC = 2, 2
    me = lax.axis_index("col")
    mr = lax.axis_index("row")
    other = 1 - mr

    def to_col(i):
        return lax.rem(me + i, C)

    def rcopy(src, dst, ssem, rsem, where):
        return pltpu.make_async_remote_copy(
            src_ref=src,
            dst_ref=dst,
            send_sem=ssem,
            recv_sem=rsem,
            device_id=where,
            device_id_type=pl.DeviceIdType.MESH,
        )

    def row_send(src, dst, sem):
        copy = rcopy(src, dst, sx.at[sem], rx.at[sem], {"row": other})
        copy.start()
        return copy

    barrier = pltpu.get_barrier_semaphore()
    for i in range(1, C):
        pl.semaphore_signal(
            barrier, inc=1, device_id={"col": to_col(i)}, device_id_type=pl.DeviceIdType.MESH
        )
    pl.semaphore_signal(
        barrier, inc=1, device_id={"row": other}, device_id_type=pl.DeviceIdType.MESH
    )
    tile = lambda p: sidx_in.at[:, pl.ds(pl.multiple_of(p * S // T * T, T), T)]
    own_idx = pltpu.make_async_copy(tile(me), iland.at[me], loc.at[0])
    own_idx.start()
    cp_up = pltpu.make_async_copy(wup, wraw, loc.at[1])
    cp_dn = pltpu.make_async_copy(wdn, wd, loc.at[2])
    own_rows = pltpu.make_async_copy(uniq.at[me], land.at[me], loc.at[3])
    own_rows.start()
    small = [
        pltpu.make_async_copy(a, b, loc.at[4 + n])
        for n, (a, b) in enumerate(
            (
                (rid_in, rid),
                (fmp_in, fmp),
                (gain_in, gain),
                (wlc_in, wlc),
                (wres_in, wres),
                (og_in, og),
                (cot_in, cot),
                (m2_in, m2_out),
            )
        )
    ]
    for cp in small:
        cp.start()
    cp_m1 = pltpu.make_async_copy(m1_in, m1_out, loc.at[12])
    cp_up.start()
    cp_dn.start()
    cp_m1.start()
    pl.semaphore_wait(barrier, C)

    order = sorted(range(1, C), key=lambda i: -min(i, C - i))
    for i in order:
        p = to_col(i)
        rcopy(tile(p), iland.at[me], sa.at[0], ra.at[0], {"col": p}).start()
    for i in order:
        p = to_col(i)
        rcopy(uniq.at[p], land.at[me], sa.at[1], ra.at[1], {"col": p}).start()
    most = pl.ds(0, C - 1)
    all_idx = rcopy(iland.at[most], iland.at[most], sa.at[0], ra.at[0], {"row": other})
    all_rows = rcopy(land.at[most], land.at[most], sa.at[1], ra.at[1], {"row": other})
    c_copy = row_send(cot_in.at[:, pl.ds(0, 8 * E)], cpeer, 0)
    rid_copy = row_send(rid_in, ridp, 12)

    to, at = iota((256, 256), 0), iota((256, 256), 1)
    perm = (((to & 31) * 8 + (to >> 5)) == at).astype(F32).astype(BF16)
    for cp in small:
        cp.wait()
    cp_up.wait()
    for g in range(4):
        blk = matmul(perm, wraw[g * 256 : (g + 1) * 256, :]).astype(BF16)
        for k in range(K):
            wp[k * T + g * 32 : k * T + (g + 1) * 32, :] = blk[k * 32 : (k + 1) * 32, :]
    lane = iota((K, K * T), 1)
    spread = jnp.where((lane & 7) == iota((K, K * T), 0), gain[...], 0.0)
    fold = ((iota((K * T, T), 0) >> 3) == iota((K * T, T), 1)).astype(F32)
    gk = matmul(spread, fold, precision=HIGH)

    amat = jnp.concatenate(
        [
            fmp[...].astype(F32),
            wlc[...].astype(F32),
            wres[...].astype(F32),
        ],
        0,
    )
    for j in range(32):
        arep[j * S : (j + 1) * S, :] = jnp.broadcast_to(amat[j : j + 1, :], (S, T))

    place = (iota((C, T), 0) == (iota((C, T), 1) >> 3)).astype(F32)
    same = iota((D, U, T), 1) == (iota((D, U, T), 2) & (U - 1))

    def labels_of(ids):
        wide = matmul(ids[...].astype(F32).reshape(D * U, C), place, precision=HIGH)
        return jnp.sum(jnp.where(same, wide.reshape(D, U, T), 0.0), 1).astype(jnp.int32)

    labels = labels_of(rid)
    target = iota((T, T), 0)
    for i in range(2):
        local = labels - (mr if i == 0 else other) * T
        for d in range(D):
            oh[i, d] = jnp.where(
                target == jnp.broadcast_to(local[d : d + 1, :], (T, T)), 1.0, 0.0
            ).astype(BF16)

    own_idx.wait()
    all_idx.wait_recv()
    ix = iland[...].astype(F32).reshape(T, T)
    mine = lax.rem(me, T // S) * S
    tiled = (iota((T, T), 0) == (iota((T, T), 1) & (S - 1)) + mine).astype(F32)
    idx_n = matmul(ix, tiled, precision=HIGH)
    idxn[...] = idx_n
    idx_t = idx_n.T
    for u in range(U):
        for q in range(4):
            lm[q * T : (q + 1) * T, u * T : (u + 1) * T] = jnp.where(
                idx_t == float(u), arep[q * T : (q + 1) * T, :], 0.0
            ).astype(BF16)
    entry = iota((U, T), 0).astype(F32)

    def fill(src, at, slots=range(0, T, 2)):
        for t in slots:
            rows = [
                jnp.where(
                    jnp.broadcast_to(idxn[v : v + 1, :], (U, T)) == entry,
                    jnp.broadcast_to(src[v : v + 1, :], (U, T)),
                    0.0,
                )
                for v in (t, t + 1)
            ]
            lmask[t // D, t % D * U : (t % D + 2) * U, at * T : (at + 1) * T] = jnp.concatenate(
                rows, 0
            ).astype(BF16)

    for q in range(4):
        ggr[...] = arep[q * T : (q + 1) * T, :].T
        fill(ggr, (q + 3) & 3)
    upstream = cot[...].astype(F32)
    for o in range(16):
        rmat[(8 + o) * S : (9 + o) * S, :] = upstream[:, o * E : (o + 1) * E].astype(BF16)

    rid_copy.wait_recv()
    local = labels_of(ridp) - mr * T
    for d in range(4):
        ohp[d] = jnp.where(
            target == jnp.broadcast_to(local[d + 4 : d + 5, :], (T, T)), 1.0, 0.0
        ).astype(BF16)
    pr[4:D, 0:T, :] = jnp.zeros((4, T, T), BF16)
    own_rows.wait()
    all_rows.wait_recv()
    t32[...] = land[...].astype(F32).reshape(T, U * E)
    for u in range(U):
        tst[u * T : (u + 1) * T, :] = t32[:, u * E : (u + 1) * E].astype(BF16)

    comp = matmul(lm[0:T, :], tst[...]).astype(BF16)
    rmat[512:640, :] = comp
    z = matmul(comp, tst[...], NT)
    gram = jnp.where(idx_t == 0.0, z[:, 0:T], 0.0)
    for u in range(1, U):
        gram = gram + jnp.where(idx_t == float(u), z[:, u * T : (u + 1) * T], 0.0)
    n_flat = float(K * T)
    g3 = gram.reshape(K, S, T)
    mu = jnp.sum(jnp.sum(g3, 0), -1, keepdims=True) / n_flat
    cent = g3 - mu[None]
    inv_in = lax.rsqrt(jnp.sum(jnp.sum(cent * cent, 0), -1, keepdims=True) / n_flat + 1e-05)
    normed_in = cent * inv_in[None]
    nrm[...] = normed_in.reshape(K * S, T)
    for k in range(K):
        nall[0, :, k * T : (k + 1) * T] = (normed_in[k] * gk[k : k + 1, :]).astype(BF16)
    n_copy = row_send(nall.at[0], nall.at[1], 1)

    y[...] = matmul(lm[T:512, :], tst[...])
    gain_out = og[...]
    c_copy.wait_recv()
    c32[0:S, :] = upstream[:, 0 : 8 * E]
    c32[S : 2 * S, :] = cpeer[...].astype(F32)
    up_fm = jnp.concatenate([c32[:, o * E : (o + 1) * E] for o in range(8)], 0) * gain_out
    up_mean = jnp.mean(up_fm, -1, keepdims=True)
    cp_dn.wait()
    n_copy.wait_recv()
    hp = matmul(nall[...].reshape(2 * S, K * T), wp[...])
    sg = jax.nn.sigmoid(hp)
    hid = (hp * sg).astype(BF16)
    f_copies = []
    for c in range(FC):
        cols = slice(c * 8 * E // FC, (c + 1) * 8 * E // FC)
        fp = matmul(hid, wd[:, cols])
        fm[:, cols] = fp
        fsend[c, 0:S] = fp[S : 2 * S].astype(BF16)
        fsend[c, S : 2 * S] = fp[0:S].astype(BF16)
        f_copies.append(row_send(fsend.at[c], frecv.at[c], 2 + c))
    ds[...] = sg * (1.0 + hp * (1.0 - sg))

    def out_norm(joined, o):
        up = upstream[:, o * E : (o + 1) * E]
        c = joined - jnp.mean(joined, -1, keepdims=True)
        inv = lax.rsqrt(jnp.mean(c * c, -1, keepdims=True) + 1e-05)
        nr = c * inv
        return nr, norm_back(up * gain_out, nr, inv)

    for o in range(8, 16):
        nr, gj = out_norm(y[(o - 8) * S : (o - 7) * S, :], o)
        lay32[:, o * E : (o + 1) * E] = nr * gain_out + y[(8 + o) * S : (9 + o) * S, :]
        rmat[(o - 8) * S : (o - 7) * S, :] = gj.astype(BF16)

    normed_fm, gh = [], None
    per = 8 // FC
    for c in range(FC):
        f_copies[c].wait_recv()
        cols = slice(c * per * E, (c + 1) * per * E)
        rows = slice(c * per * 2 * S, (c + 1) * per * 2 * S)
        fm[:, cols] += frecv[c].astype(F32)
        joined = jnp.concatenate(
            [fm[:, o * E : (o + 1) * E] for o in range(c * per, (c + 1) * per)], 0
        )
        cen = joined - jnp.mean(joined, -1, keepdims=True)
        inv_fm = lax.rsqrt(jnp.mean(cen * cen, -1, keepdims=True) + 1e-05)
        normed = cen * inv_fm
        across = jnp.mean(up_fm[rows] * cen, -1, keepdims=True) * inv_fm
        grad_fm = (up_fm[rows] - up_mean[rows] - normed * across) * inv_fm
        for o in range(per):
            at = (c * per + o) * E
            gf32[:, at : at + E] = grad_fm[o * 2 * S : (o + 1) * 2 * S]
            normed_fm.append(normed[o * 2 * S : o * 2 * S + S])
        part = matmul(gf32[:, cols].astype(BF16), wd[:, cols], NT)
        gh = part if gh is None else gh + part
    gp = (gh * ds[...]).astype(BF16)
    q_copies = []
    for c in range(QC):
        cols = slice(c * K * T // QC, (c + 1) * K * T // QC)
        part = matmul(gp, wp[cols, :], NT)
        gq[:, cols] = part[0:S]
        qsend[c] = part[S : 2 * S].astype(BF16)
        q_copies.append(row_send(qsend.at[c], qrecv.at[c], 2 + FC + c))
    for o in range(8):
        lay32[:, o * E : (o + 1) * E] = (
            normed_fm[o] * gain_out + y[(8 + o) * S : (9 + o) * S, :]
        )
    lay_out[...] = lay32[...].astype(BF16)
    lge[...] = matmul(
        lmask[:, :, 0:384].reshape(C * D * U, 384), rmat[0:384, :]
    ).reshape(C, D * U, E)
    for c in range(QC):
        q_copies[c].wait_recv()
    width = K // QC
    qs = [
        (
            gq[:, k * T : (k + 1) * T]
            + qrecv[k // width, :, k % width * T : (k % width + 1) * T].astype(F32)
        )
        * gk[k : k + 1, :]
        for k in range(K)
    ]
    ns = [nrm[k * S : (k + 1) * S, :] for k in range(K)]
    first = jnp.sum(sum(qs), -1, keepdims=True) / n_flat
    second = jnp.sum(sum(q * n for q, n in zip(qs, ns)), -1, keepdims=True) / n_flat
    for k in range(K):
        ggr[k * S : (k + 1) * S, :] = (qs[k] - first - ns[k] * second) * inv_in
    gg = ggr[...]
    for u in range(U):
        lm[0:T, u * T : (u + 1) * T] = jnp.where(idx_t == float(u), gg, 0.0).astype(BF16)
    ggr[...] = gg.T
    rmat[384:512, :] = matmul(lm[0:T, :], tst[...]).astype(BF16)

    units = []

    def col_send(src, dst, sem):
        for i in order:
            p = to_col(i)
            rcopy(src(p), dst, sa.at[sem], ra.at[sem], {"col": p}).start()

    def unit_send(j, row):
        cut = pl.ds(row, 16)
        col_send(lambda p: sb.at[p, cut], rland.at[me, cut], 2 + j)
        units.append(
            rcopy(
                sb.at[most, cut], rland.at[most, cut], sa.at[2 + j], ra.at[2 + j], {"row": other}
            )
        )

    y_copies = []
    for half in (1, 0):
        at = half * 32
        fill(ggr, 4, [t for t in range(0, T, 2) if t % D // 4 == half])
        part = matmul(lmask[:, at : at + 32, 384:640].reshape(C * 32, 256), rmat[384:640, :])
        part = part.reshape(C, 32, E) + lge[:, at : at + 32, :]
        row = half * 48
        top = part[:, :, T:E]
        sb[:, row : row + 16, :] = jnp.concatenate([top[:, :16], top[:, 16:]], -1).astype(BF16)
        sb[:, row + 16 : row + 48, :] = part[:, :, 0:T].astype(BF16)
        if half:
            for c in range(2):
                y_copies.append(
                    row_send(
                        sb.at[:, pl.ds(64 + c * 16, 16)], yb.at[:, pl.ds(c * 16, 16)], 10 + c
                    )
                )
            unit_send(0, 48)
        else:
            for j in range(3):
                unit_send(1 + j, j * 16)
    late = pl.ds(64, 32)
    col_send(lambda p: sb.at[p, late], rland.at[me, late], 6)
    lists = [
        rcopy(sb.at[most, late], rland.at[most, late], sa.at[6], ra.at[6], {"row": other})
    ]
    rland[me] = sb[me]

    def relay(c):
        y_copies[c].wait_recv()
        cut = pl.ds(c * 16, 16)
        col_send(lambda p: yb.at[p, cut], rlandp.at[me, cut], 7 + c)
        rlandp[me, c * 16 : (c + 1) * 16, :] = yb[me, c * 16 : (c + 1) * 16, :]
        lists.append(
            rcopy(yb.at[most, cut], rlandp.at[most, cut], sa.at[7 + c], ra.at[7 + c], {"row": other})
        )

    def halves(ref, row):
        both = ref[:, row : row + 16, :].astype(F32)
        return [both[:, h * U : (h + 1) * U, :].reshape(T, T).T.astype(BF16) for h in range(2)]

    p_copies = []
    for j in range(4):
        if j < 2:
            relay(j)
        units[j].wait_recv()
        base, row = ((4, 48), (0, 0), (0, 16), (2, 32))[j]
        pieces = []
        for h, x in enumerate(halves(rland, row)):
            if j < 2:
                pieces.append((base + h, T, E, x[: E - T]))
                pieces.append((base + 2 + h, T, E, x[E - T :]))
            else:
                pieces.append((base + h, 0, T, x))
        for d, a, b, x in pieces:
            ps[d, a:b, :] = matmul(x, oh[1, d], NT).astype(BF16)
        part = (pl.ds(base, 4), pl.ds(T, E - T)) if j < 2 else (pl.ds(base, 2), pl.ds(0, T))
        p_copies.append(row_send(ps.at[part], pr.at[part], 2 + FC + QC + j))
        for d, a, b, x in pieces:
            rg_out[d, a:b, :] = matmul(x, oh[0, d], NT)
    lists[0].wait_recv()
    for c in range(2):
        for h, x in enumerate(halves(rland, 64 + c * 16)):
            d = 4 + 2 * c + h
            rg_out[d, 0:T, :] = matmul(x, oh[0, d], NT)
    for c in range(2):
        lists[1 + c].wait_recv()
        for h, x in enumerate(halves(rlandp, c * 16)):
            d = 4 + 2 * c + h
            rg_out[d, 0:T, :] += matmul(x, ohp[d - 4], NT)
    cp_m1.wait()
    for cp in p_copies:
        cp.wait_recv()
    for cp in (
        all_idx,
        all_rows,
        c_copy,
        n_copy,
        *f_copies,
        *q_copies,
        rid_copy,
        *units,
        *y_copies,
        *lists,
        *p_copies,
    ):
        cp.wait_send()


def moment_kernel(
    width, lay, own, got, m1, m2, lay_out, m1_out, m2_out, step_out, mv, sv, m2v, sem
):
    D = own.shape[0]
    copies = [pltpu.make_async_copy(lay, lay_out, sem.at[0])]
    copies[0].start()
    for d in range(D):
        g = own[d] + got[d].astype(F32)
        first = 0.9 * m1[d] + 0.1 * g
        second = 0.99 * m2[d : d + 1, :] + 0.01 * (jnp.sum(g * g, 0, keepdims=True) / width)
        mv[d] = first
        m2v[d : d + 1, :] = second
        sv[d] = first * lax.rsqrt(second)
        for n, (a, b) in enumerate(((mv, m1_out), (sv, step_out))):
            copies.append(pltpu.make_async_copy(a.at[d], b.at[d], sem.at[2 + 2 * d + n]))
            copies[-1].start()
    copies.append(pltpu.make_async_copy(m2v, m2_out, sem.at[1]))
    copies[-1].start()
    for cp in copies:
        cp.wait()


def fast_body(
    C,
    R,
    uniq_rows,
    row_ids,
    sample_idx,
    fm_proj,
    ln_gain,
    w_up,
    w_down,
    w_lc,
    w_res,
    out_gain,
    cotangent,
    moment1,
    moment2,
):
    D = uniq_rows.shape[1]
    S = cotangent.shape[0]
    hid = w_up.shape[1]
    wide = w_down.shape[1]
    flat = w_up.shape[0]
    width = out_gain.shape[0]
    T = C * D
    vmem = pl.BlockSpec(memory_space=pltpu.VMEM)
    hbm = pl.BlockSpec(memory_space=pl.ANY)
    dma = pltpu.SemaphoreType.DMA
    layer_out, own, got, m1, m2 = pl.pallas_call(
        functools.partial(fused_kernel, C, D),
        out_shape=(
            pltpu.VMEM((S, 16 * width), BF16),
            pltpu.VMEM((D, width, T), F32),
            pltpu.VMEM((D, width, T), BF16),
            pltpu.VMEM((D, width, T), F32),
            pltpu.VMEM((D, T), F32),
        ),
        in_specs=[hbm] * 13,
        out_specs=(vmem,) * 5,
        scratch_shapes=[
            pltpu.VMEM((D, 8, C), jnp.int32),
            pltpu.VMEM((8, T), BF16),
            pltpu.VMEM((1, flat), F32),
            pltpu.VMEM((8, T), BF16),
            pltpu.VMEM((16, T), BF16),
            pltpu.VMEM((1, width), F32),
            pltpu.VMEM((S, 16 * width), BF16),
            pltpu.VMEM((S, wide), BF16),
            pltpu.VMEM((C, D, wide), BF16),
            pltpu.VMEM((C, D, T), jnp.int32),
            pltpu.VMEM((flat, hid), BF16),
            pltpu.VMEM((flat, hid), BF16),
            pltpu.VMEM((hid, wide), BF16),
            pltpu.VMEM((T, wide), F32),
            pltpu.VMEM((8 * T, width), BF16),
            pltpu.VMEM((512, 8 * T), BF16),
            pltpu.VMEM((C, 8 * D, 640), BF16),
            pltpu.VMEM((512, T), F32),
            pltpu.VMEM((640, width), BF16),
            pltpu.VMEM((128, T), F32),
            pltpu.VMEM((128, T), F32),
            pltpu.VMEM((T, 128), F32),
            pltpu.VMEM((2, S, flat), BF16),
            pltpu.VMEM((384, width), F32),
            pltpu.VMEM((2 * S, hid), F32),
            pltpu.VMEM((2 * S, wide), F32),
            pltpu.VMEM((2, 2 * S, wide // 2), BF16),
            pltpu.VMEM((2, 2 * S, wide // 2), BF16),
            pltpu.VMEM((2 * S, wide), F32),
            pltpu.VMEM((2, S, flat // 2), BF16),
            pltpu.VMEM((2, S, flat // 2), BF16),
            pltpu.VMEM((S, flat), F32),
            pltpu.VMEM((S, 16 * width), F32),
            pltpu.VMEM((2 * S, wide), F32),
            pltpu.VMEM((C, 8 * D, width), F32),
            pltpu.VMEM((C, 12 * D, T), BF16),
            pltpu.VMEM((C, 12 * D, T), BF16),
            pltpu.VMEM((2, D, T, T), BF16),
            pltpu.VMEM((D, width, T), BF16),
            pltpu.VMEM((D, 8, C), jnp.int32),
            pltpu.VMEM((C, 4 * D, T), BF16),
            pltpu.VMEM((C, 4 * D, T), BF16),
            pltpu.VMEM((4, T, T), BF16),
            dma((13,)),
            dma((9,)),
            dma((9,)),
            dma((13,)),
            dma((13,)),
        ],
        compiler_params=pltpu.CompilerParams(
            collective_id=0, has_side_effects=True, vmem_limit_bytes=36 * 1024 * 1024
        ),
        name="wukong_step",
    )(
        *(
            pltpu.with_memory_space_constraint(a, pltpu.HBM)
            for a in (
                uniq_rows,
                row_ids.transpose(1, 2, 0),
                sample_idx.T,
                fm_proj.T,
                ln_gain.reshape(1, flat),
                w_up,
                w_down,
                w_lc,
                w_res,
                out_gain.reshape(1, width),
                cotangent,
                moment1.transpose(0, 2, 1),
                moment2,
            )
        )
    )
    layer_out, own, got, m1, m2 = (
        pltpu.with_memory_space_constraint(a, pltpu.VMEM) for a in (layer_out, own, got, m1, m2)
    )
    layer_out, new_moment1, new_moment2, row_step = pl.pallas_call(
        functools.partial(moment_kernel, width),
        out_shape=(
            jax.ShapeDtypeStruct((S, 16 * width), BF16),
            jax.ShapeDtypeStruct((D, width, T), F32),
            jax.ShapeDtypeStruct((D, T), F32),
            jax.ShapeDtypeStruct((D, width, T), F32),
        ),
        in_specs=[vmem] * 5,
        out_specs=(hbm,) * 4,
        scratch_shapes=[
            pltpu.VMEM((D, width, T), F32),
            pltpu.VMEM((D, width, T), F32),
            pltpu.VMEM((D, T), F32),
            dma((2 + 2 * D,)),
        ],
        compiler_params=pltpu.CompilerParams(vmem_limit_bytes=8 * 1024 * 1024),
        name="moments",
    )(layer_out, own, got, m1, m2)
    return (
        layer_out,
        new_moment1.transpose(0, 2, 1),
        new_moment2,
        row_step.transpose(0, 2, 1),
    )


def step(C, R, *args):
    if args[0].shape[1] == 8 and C == 16 and R == 2:
        return fast_body(C, R, *args)
    return plain_body(*args)


def solution(mesh):
    return jax.shard_map(
        functools.partial(step, mesh.shape["col"], mesh.shape["row"]),
        mesh=mesh,
        in_specs=(
            P("row", "col", None),
            P("row", "col", None),
            P("row", "col"),
            P(),
            P(),
            P(None, "row"),
            P("row", None),
            P(),
            P(),
            P(),
            P(("row", "col"), None),
            P("col", "row", None),
            P("col", "row"),
        ),
        out_specs=(
            P(("row", "col"), None),
            P("col", "row", None),
            P("col", "row"),
            P("col", "row", None),
        ),
        check_vma=False,
    )
```

```python
import functools

import jax
import jax.numpy as jnp
from jax import lax
from jax.experimental import pallas as pl
from jax.experimental.pallas import tpu as pltpu
from jax.sharding import PartitionSpec as P

HIGH = lax.Precision.HIGHEST


def layer_norm(values, gain):
    centered = values - jnp.mean(values, -1, keepdims=True)
    inverse = lax.rsqrt(jnp.mean(centered * centered, -1, keepdims=True) + 1e-05)
    normed = centered * inverse
    return (normed * gain, normed, inverse)


def norm_back(grad_out, normed, inverse):
    first = jnp.mean(grad_out, -1, keepdims=True)
    second = jnp.mean(grad_out * normed, -1, keepdims=True)
    return (grad_out - first - normed * second) * inverse


def silu_grad(values):
    sigma = jax.nn.sigmoid(values)
    return sigma * (1.0 + values * (1.0 - sigma))


def plain_body(
    uniq_rows,
    row_ids,
    sample_idx,
    fm_proj,
    ln_gain,
    w_up,
    w_down,
    w_lc,
    w_res,
    out_gain,
    cotangent,
    moment1,
    moment2,
):
    columns = lax.axis_size("col")
    owners = lax.axis_size("row")
    slot_dev = uniq_rows.shape[1]
    width = out_gain.shape[0]
    uniq = uniq_rows.shape[2] // width
    samples = cotangent.shape[0]
    slots = slot_dev * columns
    vocab_dev = moment2.shape[1]
    rank = fm_proj.shape[1]
    fm_rows = w_down.shape[1] // width
    out_rows = w_res.shape[0]
    entry_iota = jnp.arange(uniq, dtype=jnp.int32)
    index_local = sample_idx.reshape(columns, samples, slot_dev)
    index = lax.all_to_all(index_local, "col", split_axis=0, concat_axis=2, tiled=True).reshape(
        samples, slots
    )
    picker = (index[:, :, None] == entry_iota).astype(jnp.bfloat16)
    moved = lax.all_to_all(uniq_rows, "col", split_axis=0, concat_axis=1, tiled=True)
    table = moved.reshape(slots, uniq, width)
    embed = jnp.einsum("stl,tle->ste", picker, table, preferred_element_type=jnp.float32).astype(
        jnp.bfloat16
    )
    compress = jnp.einsum("ste,tk->sek", embed, fm_proj, preferred_element_type=jnp.float32).astype(
        jnp.bfloat16
    )
    gram = jnp.einsum("ste,sek->stk", embed, compress, preferred_element_type=jnp.float32)
    flat = gram.reshape(samples, slots * rank)
    scaled, normed_in, inverse_in = layer_norm(flat, ln_gain)
    normal_in = scaled.astype(jnp.bfloat16)
    hidden_pre = jnp.dot(
        lax.all_gather(normal_in, "row", axis=0, tiled=True),
        w_up,
        preferred_element_type=jnp.float32,
    )
    hidden = jax.nn.silu(hidden_pre).astype(jnp.bfloat16)
    part_rows = hidden
    fm_out = lax.psum_scatter(
        jnp.dot(part_rows, w_down, preferred_element_type=jnp.float32),
        "row",
        scatter_dimension=0,
        tiled=True,
    )
    linear = jnp.einsum("lt,ste->sle", w_lc, embed, preferred_element_type=jnp.float32)
    joined = jnp.concatenate([fm_out.reshape(samples, fm_rows, width), linear], 1)
    normed_out, normed_rows, inverse_rows = layer_norm(joined, out_gain)
    residual = jnp.einsum("ot,ste->soe", w_res, embed, preferred_element_type=jnp.float32)
    layer_out = (normed_out + residual).reshape(samples, out_rows * width).astype(jnp.bfloat16)
    upstream = cotangent.astype(jnp.float32).reshape(samples, out_rows, width)
    grad_joined = norm_back(upstream * out_gain, normed_rows, inverse_rows)
    grad_fm = grad_joined[:, :fm_rows].reshape(samples, fm_rows * width).astype(jnp.bfloat16)
    grad_hidden = lax.dot_general(
        lax.all_gather(grad_fm, "row", axis=0, tiled=True),
        w_down,
        (((1,), (1,)), ((), ())),
        preferred_element_type=jnp.float32,
    )
    grad_pre = (grad_hidden * silu_grad(hidden_pre)).astype(jnp.bfloat16)
    part_rows = grad_pre
    grad_flat = lax.psum_scatter(
        lax.dot_general(
            part_rows, w_up, (((1,), (1,)), ((), ())), preferred_element_type=jnp.float32
        ).astype(jnp.bfloat16),
        "row",
        scatter_dimension=0,
        tiled=True,
    ).astype(jnp.float32)
    grad_gram = norm_back(grad_flat * ln_gain, normed_in, inverse_in).reshape(samples, slots, rank)
    grad_embed = jnp.einsum("stk,sek->ste", grad_gram, compress.astype(jnp.float32), precision=HIGH)
    grad_comp = jnp.einsum(
        "ste,stk->sek", embed, grad_gram, precision=HIGH, preferred_element_type=jnp.float32
    )
    grad_embed = grad_embed + jnp.einsum(
        "tk,sek->ste", fm_proj.astype(jnp.float32), grad_comp, precision=HIGH
    )
    grad_embed = grad_embed + jnp.einsum(
        "lt,sle->ste", w_lc.astype(jnp.float32), grad_joined[:, fm_rows:], precision=HIGH
    )
    grad_embed = grad_embed + jnp.einsum(
        "ot,soe->ste", w_res.astype(jnp.float32), upstream, precision=HIGH
    )
    list_grads = jnp.einsum("stl,ste->tle", picker.astype(jnp.float32), grad_embed, precision=HIGH)
    returned = lax.all_to_all(
        list_grads.reshape(columns, slot_dev, uniq * width),
        "col",
        split_axis=0,
        concat_axis=0,
        tiled=True,
    )
    entry_grads = returned.reshape(columns * slot_dev * uniq, width)
    row_list = row_ids.reshape(-1)
    slot_of = jnp.broadcast_to(
        jnp.arange(slot_dev, dtype=jnp.int32)[None, :, None], row_ids.shape
    ).reshape(-1)
    owner = row_list // vocab_dev
    target = slot_of * vocab_dev + row_list % vocab_dev
    span = slot_dev * vocab_dev
    entries = row_list.shape[0]
    capacity = 5 * entries // (4 * owners)
    onehot = (owner[:, None] == jnp.arange(owners, dtype=jnp.int32)).astype(jnp.int32)
    before = jnp.cumsum(onehot, 0) - onehot
    place = jnp.sum(before * onehot, 1)
    target_slot = owner * capacity + place
    bucket = jnp.zeros((owners * capacity, width), jnp.float32).at[target_slot].set(entry_grads)
    labels = (
        jnp.full((owners * capacity,), -1.0, jnp.float32)
        .at[target_slot]
        .set(target.astype(jnp.float32))
    )
    got_rows, got_labels = (
        lax.all_to_all(
            bucket.reshape(owners, capacity, width), "row", split_axis=0, concat_axis=0, tiled=True
        ),
        lax.all_to_all(
            labels.reshape(owners, capacity), "row", split_axis=0, concat_axis=0, tiled=True
        ),
    )
    segment = jnp.where(got_labels >= 0.0, got_labels, float(span)).astype(jnp.int32).reshape(-1)
    summed = jax.ops.segment_sum(got_rows.reshape(-1, width), segment, num_segments=span + 1)[:span]
    row_grads = summed.reshape(slot_dev, vocab_dev, width)
    new_moment1 = 0.9 * moment1 + 0.1 * row_grads
    new_moment2 = 0.99 * moment2 + 0.01 * jnp.mean(row_grads * row_grads, -1)
    row_step = new_moment1 * lax.rsqrt(new_moment2)[..., None]
    return (layer_out, new_moment1, new_moment2, row_step)


F32 = jnp.float32
BF16 = jnp.bfloat16
NT = (((1,), (1,)), ((), ()))


def iota(shape, dim):
    return lax.broadcasted_iota(jnp.int32, shape, dim)


def matmul(a, b, dims=(((1,), (0,)), ((), ())), precision=None):
    return lax.dot_general(a, b, dims, precision=precision, preferred_element_type=F32)


def fused_kernel(
    C,
    D,
    uniq,
    rid_in,
    sidx_in,
    fmp_in,
    gain_in,
    wup,
    wdn,
    wlc_in,
    wres_in,
    og_in,
    cot_in,
    m1_in,
    m2_in,
    lay_out,
    rg_out,
    pr,
    m1_out,
    m2_out,
    rid,
    sidx,
    fmp,
    gain,
    wlc,
    wres,
    og,
    cot,
    cpeer,
    isend,
    land,
    iland,
    wraw,
    wp,
    wd,
    t32,
    tst,
    lm,
    lmask,
    arep,
    rmat,
    nrm,
    ggr,
    idxn,
    nall,
    y,
    ds,
    c32,
    fsend,
    frecv,
    fm,
    qsend,
    qrecv,
    gq,
    lay32,
    gf32,
    lge,
    sb,
    rland,
    oh,
    ps,
    ridp,
    yb,
    rlandp,
    ohp,
    loc,
    sa,
    ra,
    sx,
    rx,
):
    S, E, U, K, T = 16, 192, 8, 8, 128
    FC, QC = 2, 2
    me = lax.axis_index("col")
    mr = lax.axis_index("row")
    other = 1 - mr

    def to_col(i):
        return lax.rem(me + i, C)

    def rcopy(src, dst, ssem, rsem, where):
        return pltpu.make_async_remote_copy(
            src_ref=src,
            dst_ref=dst,
            send_sem=ssem,
            recv_sem=rsem,
            device_id=where,
            device_id_type=pl.DeviceIdType.MESH,
        )

    def row_send(src, dst, sem):
        copy = rcopy(src, dst, sx.at[sem], rx.at[sem], {"row": other})
        copy.start()
        return copy

    barrier = pltpu.get_barrier_semaphore()
    for i in range(1, C):
        pl.semaphore_signal(
            barrier, inc=1, device_id={"col": to_col(i)}, device_id_type=pl.DeviceIdType.MESH
        )
    pl.semaphore_signal(
        barrier, inc=1, device_id={"row": other}, device_id_type=pl.DeviceIdType.MESH
    )
    cp_idx = pltpu.make_async_copy(sidx_in, sidx, loc.at[0])
    cp_idx.start()
    cp_up = pltpu.make_async_copy(wup, wraw, loc.at[1])
    cp_dn = pltpu.make_async_copy(wdn, wd, loc.at[2])
    own_rows = pltpu.make_async_copy(uniq.at[me], land.at[me], loc.at[3])
    own_rows.start()
    small = [
        pltpu.make_async_copy(a, b, loc.at[4 + n])
        for n, (a, b) in enumerate(
            (
                (rid_in, rid),
                (fmp_in, fmp),
                (gain_in, gain),
                (wlc_in, wlc),
                (wres_in, wres),
                (og_in, og),
                (cot_in, cot),
                (m2_in, m2_out),
            )
        )
    ]
    for cp in small:
        cp.start()
    cp_m1 = pltpu.make_async_copy(m1_in, m1_out, loc.at[12])
    cp_up.start()
    cp_dn.start()
    cp_m1.start()
    wide = C * S
    fold_s = ((iota((wide, T), 0) & (S - 1)) == (iota((wide, T), 1) & (S - 1))).astype(F32)
    of_peer = (iota((C, wide), 1) >> 4) == iota((C, wide), 0)
    cp_idx.wait()
    listed = sidx[...].astype(F32)
    spread_d = [
        jnp.where(of_peer, jnp.broadcast_to(listed[d : d + 1, :], (C, wide)), 0.0) for d in range(D)
    ]
    spread_d = matmul(jnp.concatenate(spread_d, 0).astype(BF16), fold_s.astype(BF16))
    spread_d = spread_d.reshape(D, C, T)
    packed = jnp.sum(
        jnp.where((iota((D, C, T), 2) >> 4) == iota((D, C, T), 0), spread_d, 0.0), 0
    ).astype(jnp.int32)
    for p in range(C):
        isend[p] = packed[p : p + 1, :]
    iland[me] = isend[me]
    pl.semaphore_wait(barrier, C)

    order = sorted(range(1, C), key=lambda i: -min(i, C - i))
    for i in order:
        p = to_col(i)
        rcopy(isend.at[p], iland.at[me], sa.at[0], ra.at[0], {"col": p}).start()
    for i in order:
        p = to_col(i)
        rcopy(uniq.at[p], land.at[me], sa.at[1], ra.at[1], {"col": p}).start()
    most = pl.ds(0, C - 1)
    all_idx = rcopy(iland.at[most], iland.at[most], sa.at[0], ra.at[0], {"row": other})
    all_rows = rcopy(land.at[most], land.at[most], sa.at[1], ra.at[1], {"row": other})
    c_copy = row_send(cot_in.at[:, pl.ds(0, 8 * E)], cpeer, 0)
    rid_copy = row_send(rid_in, ridp, 12)

    to, at = iota((256, 256), 0), iota((256, 256), 1)
    perm = (((to & 31) * 8 + (to >> 5)) == at).astype(F32).astype(BF16)
    for cp in small:
        cp.wait()
    cp_up.wait()
    for g in range(4):
        blk = matmul(perm, wraw[g * 256 : (g + 1) * 256, :]).astype(BF16)
        for k in range(K):
            wp[k * T + g * 32 : k * T + (g + 1) * 32, :] = blk[k * 32 : (k + 1) * 32, :]
    lane = iota((K, K * T), 1)
    spread = jnp.where((lane & 7) == iota((K, K * T), 0), gain[...], 0.0)
    fold = ((iota((K * T, T), 0) >> 3) == iota((K * T, T), 1)).astype(F32)
    gk = matmul(spread, fold, precision=HIGH)

    amat = jnp.concatenate(
        [
            fmp[...].astype(F32),
            wlc[...].astype(F32),
            wres[...].astype(F32),
        ],
        0,
    )
    for j in range(32):
        arep[j * S : (j + 1) * S, :] = jnp.broadcast_to(amat[j : j + 1, :], (S, T))

    place = (iota((C, T), 0) == (iota((C, T), 1) >> 3)).astype(F32)
    same = iota((D, U, T), 1) == (iota((D, U, T), 2) & (U - 1))

    def labels_of(ids):
        wide = matmul(ids[...].astype(F32).reshape(D * U, C), place, precision=HIGH)
        return jnp.sum(jnp.where(same, wide.reshape(D, U, T), 0.0), 1).astype(jnp.int32)

    labels = labels_of(rid)
    target = iota((T, T), 0)
    for i in range(2):
        local = labels - (mr if i == 0 else other) * T
        for d in range(D):
            oh[i, d] = jnp.where(
                target == jnp.broadcast_to(local[d : d + 1, :], (T, T)), 1.0, 0.0
            ).astype(BF16)

    all_idx.wait_recv()
    group = (iota((D, T), 1) >> 4) == iota((D, T), 0)
    ix = [
        jnp.where(group, jnp.broadcast_to(iland[p].astype(F32), (D, T)), 0.0) for p in range(C)
    ]
    idx_n = matmul(jnp.concatenate(ix, 0).astype(BF16), fold_s[0:T].astype(BF16))
    idxn[...] = idx_n
    idx_t = idx_n.T
    for u in range(U):
        for q in range(4):
            lm[q * T : (q + 1) * T, u * T : (u + 1) * T] = jnp.where(
                idx_t == float(u), arep[q * T : (q + 1) * T, :], 0.0
            ).astype(BF16)
    entry = iota((U, T), 0).astype(F32)

    def fill(src, at, slots=range(0, T, 2)):
        for t in slots:
            rows = [
                jnp.where(
                    jnp.broadcast_to(idxn[v : v + 1, :], (U, T)) == entry,
                    jnp.broadcast_to(src[v : v + 1, :], (U, T)),
                    0.0,
                )
                for v in (t, t + 1)
            ]
            lmask[t // D, t % D * U : (t % D + 2) * U, at * T : (at + 1) * T] = jnp.concatenate(
                rows, 0
            ).astype(BF16)

    for q in range(4):
        ggr[...] = arep[q * T : (q + 1) * T, :].T
        fill(ggr, (q + 3) & 3)
    upstream = cot[...].astype(F32)
    for o in range(16):
        rmat[(8 + o) * S : (9 + o) * S, :] = upstream[:, o * E : (o + 1) * E].astype(BF16)

    rid_copy.wait_recv()
    local = labels_of(ridp) - mr * T
    for d in range(4):
        ohp[d] = jnp.where(
            target == jnp.broadcast_to(local[d + 4 : d + 5, :], (T, T)), 1.0, 0.0
        ).astype(BF16)
    pr[4:D, 0:T, :] = jnp.zeros((4, T, T), BF16)
    own_rows.wait()
    all_rows.wait_recv()
    t32[...] = land[...].astype(F32).reshape(T, U * E)
    for u in range(U):
        tst[u * T : (u + 1) * T, :] = t32[:, u * E : (u + 1) * E].astype(BF16)

    comp = matmul(lm[0:T, :], tst[...]).astype(BF16)
    rmat[512:640, :] = comp
    z = matmul(comp, tst[...], NT)
    gram = jnp.where(idx_t == 0.0, z[:, 0:T], 0.0)
    for u in range(1, U):
        gram = gram + jnp.where(idx_t == float(u), z[:, u * T : (u + 1) * T], 0.0)
    n_flat = float(K * T)
    g3 = gram.reshape(K, S, T)
    mu = jnp.sum(jnp.sum(g3, 0), -1, keepdims=True) / n_flat
    cent = g3 - mu[None]
    inv_in = lax.rsqrt(jnp.sum(jnp.sum(cent * cent, 0), -1, keepdims=True) / n_flat + 1e-05)
    normed_in = cent * inv_in[None]
    nrm[...] = normed_in.reshape(K * S, T)
    for k in range(K):
        nall[0, :, k * T : (k + 1) * T] = (normed_in[k] * gk[k : k + 1, :]).astype(BF16)
    n_copy = row_send(nall.at[0], nall.at[1], 1)

    y[...] = matmul(lm[T:512, :], tst[...])
    gain_out = og[...]
    c_copy.wait_recv()
    c32[0:S, :] = upstream[:, 0 : 8 * E]
    c32[S : 2 * S, :] = cpeer[...].astype(F32)
    up_fm = jnp.concatenate([c32[:, o * E : (o + 1) * E] for o in range(8)], 0) * gain_out
    up_mean = jnp.mean(up_fm, -1, keepdims=True)
    cp_dn.wait()
    n_copy.wait_recv()
    hp = matmul(nall[...].reshape(2 * S, K * T), wp[...])
    sg = jax.nn.sigmoid(hp)
    hid = (hp * sg).astype(BF16)
    f_copies = []
    for c in range(FC):
        cols = slice(c * 8 * E // FC, (c + 1) * 8 * E // FC)
        fp = matmul(hid, wd[:, cols])
        fm[:, cols] = fp
        fsend[c, 0:S] = fp[S : 2 * S].astype(BF16)
        fsend[c, S : 2 * S] = fp[0:S].astype(BF16)
        f_copies.append(row_send(fsend.at[c], frecv.at[c], 2 + c))
    ds[...] = sg * (1.0 + hp * (1.0 - sg))

    def out_norm(joined, o):
        up = upstream[:, o * E : (o + 1) * E]
        c = joined - jnp.mean(joined, -1, keepdims=True)
        inv = lax.rsqrt(jnp.mean(c * c, -1, keepdims=True) + 1e-05)
        nr = c * inv
        return nr, norm_back(up * gain_out, nr, inv)

    for o in range(8, 16):
        nr, gj = out_norm(y[(o - 8) * S : (o - 7) * S, :], o)
        lay32[:, o * E : (o + 1) * E] = nr * gain_out + y[(8 + o) * S : (9 + o) * S, :]
        rmat[(o - 8) * S : (o - 7) * S, :] = gj.astype(BF16)

    normed_fm, gh = [], None
    per = 8 // FC
    for c in range(FC):
        f_copies[c].wait_recv()
        cols = slice(c * per * E, (c + 1) * per * E)
        rows = slice(c * per * 2 * S, (c + 1) * per * 2 * S)
        fm[:, cols] += frecv[c].astype(F32)
        joined = jnp.concatenate(
            [fm[:, o * E : (o + 1) * E] for o in range(c * per, (c + 1) * per)], 0
        )
        cen = joined - jnp.mean(joined, -1, keepdims=True)
        inv_fm = lax.rsqrt(jnp.mean(cen * cen, -1, keepdims=True) + 1e-05)
        normed = cen * inv_fm
        across = jnp.mean(up_fm[rows] * cen, -1, keepdims=True) * inv_fm
        grad_fm = (up_fm[rows] - up_mean[rows] - normed * across) * inv_fm
        for o in range(per):
            at = (c * per + o) * E
            gf32[:, at : at + E] = grad_fm[o * 2 * S : (o + 1) * 2 * S]
            normed_fm.append(normed[o * 2 * S : o * 2 * S + S])
        part = matmul(gf32[:, cols].astype(BF16), wd[:, cols], NT)
        gh = part if gh is None else gh + part
    gp = (gh * ds[...]).astype(BF16)
    q_copies = []
    for c in range(QC):
        cols = slice(c * K * T // QC, (c + 1) * K * T // QC)
        part = matmul(gp, wp[cols, :], NT)
        gq[:, cols] = part[0:S]
        qsend[c] = part[S : 2 * S].astype(BF16)
        q_copies.append(row_send(qsend.at[c], qrecv.at[c], 2 + FC + c))
    for o in range(8):
        lay32[:, o * E : (o + 1) * E] = (
            normed_fm[o] * gain_out + y[(8 + o) * S : (9 + o) * S, :]
        )
    lay_out[...] = lay32[...].astype(BF16)
    lge[...] = matmul(
        lmask[:, :, 0:384].reshape(C * D * U, 384), rmat[0:384, :]
    ).reshape(C, D * U, E)
    for c in range(QC):
        q_copies[c].wait_recv()
    width = K // QC
    qs = [
        (
            gq[:, k * T : (k + 1) * T]
            + qrecv[k // width, :, k % width * T : (k % width + 1) * T].astype(F32)
        )
        * gk[k : k + 1, :]
        for k in range(K)
    ]
    ns = [nrm[k * S : (k + 1) * S, :] for k in range(K)]
    first = jnp.sum(sum(qs), -1, keepdims=True) / n_flat
    second = jnp.sum(sum(q * n for q, n in zip(qs, ns)), -1, keepdims=True) / n_flat
    for k in range(K):
        ggr[k * S : (k + 1) * S, :] = (qs[k] - first - ns[k] * second) * inv_in
    gg = ggr[...]
    for u in range(U):
        lm[0:T, u * T : (u + 1) * T] = jnp.where(idx_t == float(u), gg, 0.0).astype(BF16)
    ggr[...] = gg.T
    rmat[384:512, :] = matmul(lm[0:T, :], tst[...]).astype(BF16)

    units = []

    def col_send(src, dst, sem):
        for i in order:
            p = to_col(i)
            rcopy(src(p), dst, sa.at[sem], ra.at[sem], {"col": p}).start()

    def unit_send(j, row):
        cut = pl.ds(row, 16)
        col_send(lambda p: sb.at[p, cut], rland.at[me, cut], 2 + j)
        units.append(
            rcopy(
                sb.at[most, cut], rland.at[most, cut], sa.at[2 + j], ra.at[2 + j], {"row": other}
            )
        )

    y_copies = []
    for half in (1, 0):
        at = half * 32
        fill(ggr, 4, [t for t in range(0, T, 2) if t % D // 4 == half])
        part = matmul(lmask[:, at : at + 32, 384:640].reshape(C * 32, 256), rmat[384:640, :])
        part = part.reshape(C, 32, E) + lge[:, at : at + 32, :]
        row = half * 48
        top = part[:, :, T:E]
        sb[:, row : row + 16, :] = jnp.concatenate([top[:, :16], top[:, 16:]], -1).astype(BF16)
        sb[:, row + 16 : row + 48, :] = part[:, :, 0:T].astype(BF16)
        if half:
            for c in range(2):
                y_copies.append(
                    row_send(
                        sb.at[:, pl.ds(64 + c * 16, 16)], yb.at[:, pl.ds(c * 16, 16)], 10 + c
                    )
                )
            unit_send(0, 48)
        else:
            for j in range(3):
                unit_send(1 + j, j * 16)
    late = pl.ds(64, 32)
    col_send(lambda p: sb.at[p, late], rland.at[me, late], 6)
    lists = [
        rcopy(sb.at[most, late], rland.at[most, late], sa.at[6], ra.at[6], {"row": other})
    ]
    rland[me] = sb[me]

    def relay(c):
        y_copies[c].wait_recv()
        cut = pl.ds(c * 16, 16)
        col_send(lambda p: yb.at[p, cut], rlandp.at[me, cut], 7 + c)
        rlandp[me, c * 16 : (c + 1) * 16, :] = yb[me, c * 16 : (c + 1) * 16, :]
        lists.append(
            rcopy(yb.at[most, cut], rlandp.at[most, cut], sa.at[7 + c], ra.at[7 + c], {"row": other})
        )

    def halves(ref, row):
        both = ref[:, row : row + 16, :].astype(F32)
        return [both[:, h * U : (h + 1) * U, :].reshape(T, T).T.astype(BF16) for h in range(2)]

    p_copies = []
    for j in range(4):
        if j < 2:
            relay(j)
        units[j].wait_recv()
        base, row = ((4, 48), (0, 0), (0, 16), (2, 32))[j]
        pieces = []
        for h, x in enumerate(halves(rland, row)):
            if j < 2:
                pieces.append((base + h, T, E, x[: E - T]))
                pieces.append((base + 2 + h, T, E, x[E - T :]))
            else:
                pieces.append((base + h, 0, T, x))
        for d, a, b, x in pieces:
            ps[d, a:b, :] = matmul(x, oh[1, d], NT).astype(BF16)
        part = (pl.ds(base, 4), pl.ds(T, E - T)) if j < 2 else (pl.ds(base, 2), pl.ds(0, T))
        p_copies.append(row_send(ps.at[part], pr.at[part], 2 + FC + QC + j))
        for d, a, b, x in pieces:
            rg_out[d, a:b, :] = matmul(x, oh[0, d], NT)
    lists[0].wait_recv()
    for c in range(2):
        for h, x in enumerate(halves(rland, 64 + c * 16)):
            d = 4 + 2 * c + h
            rg_out[d, 0:T, :] = matmul(x, oh[0, d], NT)
    for c in range(2):
        lists[1 + c].wait_recv()
        for h, x in enumerate(halves(rlandp, c * 16)):
            d = 4 + 2 * c + h
            rg_out[d, 0:T, :] += matmul(x, ohp[d - 4], NT)
    cp_m1.wait()
    for cp in p_copies:
        cp.wait_recv()
    for cp in (
        all_idx,
        all_rows,
        c_copy,
        n_copy,
        *f_copies,
        *q_copies,
        rid_copy,
        *units,
        *y_copies,
        *lists,
        *p_copies,
    ):
        cp.wait_send()


def moment_kernel(
    width, lay, own, got, m1, m2, lay_out, m1_out, m2_out, step_out, mv, sv, m2v, sem
):
    D = own.shape[0]
    copies = [pltpu.make_async_copy(lay, lay_out, sem.at[0])]
    copies[0].start()
    for d in range(D):
        g = own[d] + got[d].astype(F32)
        first = 0.9 * m1[d] + 0.1 * g
        second = 0.99 * m2[d : d + 1, :] + 0.01 * (jnp.sum(g * g, 0, keepdims=True) / width)
        mv[d] = first
        m2v[d : d + 1, :] = second
        sv[d] = first * lax.rsqrt(second)
        for n, (a, b) in enumerate(((mv, m1_out), (sv, step_out))):
            copies.append(pltpu.make_async_copy(a.at[d], b.at[d], sem.at[2 + 2 * d + n]))
            copies[-1].start()
    copies.append(pltpu.make_async_copy(m2v, m2_out, sem.at[1]))
    copies[-1].start()
    for cp in copies:
        cp.wait()


def fast_body(
    C,
    R,
    uniq_rows,
    row_ids,
    sample_idx,
    fm_proj,
    ln_gain,
    w_up,
    w_down,
    w_lc,
    w_res,
    out_gain,
    cotangent,
    moment1,
    moment2,
):
    D = uniq_rows.shape[1]
    S = cotangent.shape[0]
    hid = w_up.shape[1]
    wide = w_down.shape[1]
    flat = w_up.shape[0]
    width = out_gain.shape[0]
    T = C * D
    vmem = pl.BlockSpec(memory_space=pltpu.VMEM)
    hbm = pl.BlockSpec(memory_space=pl.ANY)
    dma = pltpu.SemaphoreType.DMA
    layer_out, own, got, m1, m2 = pl.pallas_call(
        functools.partial(fused_kernel, C, D),
        out_shape=(
            pltpu.VMEM((S, 16 * width), BF16),
            pltpu.VMEM((D, width, T), F32),
            pltpu.VMEM((D, width, T), BF16),
            pltpu.VMEM((D, width, T), F32),
            pltpu.VMEM((D, T), F32),
        ),
        in_specs=[hbm] * 13,
        out_specs=(vmem,) * 5,
        scratch_shapes=[
            pltpu.VMEM((D, 8, C), jnp.int32),
            pltpu.VMEM((D, C * S), jnp.int32),
            pltpu.VMEM((8, T), BF16),
            pltpu.VMEM((1, flat), F32),
            pltpu.VMEM((8, T), BF16),
            pltpu.VMEM((16, T), BF16),
            pltpu.VMEM((1, width), F32),
            pltpu.VMEM((S, 16 * width), BF16),
            pltpu.VMEM((S, wide), BF16),
            pltpu.VMEM((C, 1, T), jnp.int32),
            pltpu.VMEM((C, D, wide), BF16),
            pltpu.VMEM((C, 1, T), jnp.int32),
            pltpu.VMEM((flat, hid), BF16),
            pltpu.VMEM((flat, hid), BF16),
            pltpu.VMEM((hid, wide), BF16),
            pltpu.VMEM((T, wide), F32),
            pltpu.VMEM((8 * T, width), BF16),
            pltpu.VMEM((512, 8 * T), BF16),
            pltpu.VMEM((C, 8 * D, 640), BF16),
            pltpu.VMEM((512, T), F32),
            pltpu.VMEM((640, width), BF16),
            pltpu.VMEM((128, T), F32),
            pltpu.VMEM((128, T), F32),
            pltpu.VMEM((T, 128), F32),
            pltpu.VMEM((2, S, flat), BF16),
            pltpu.VMEM((384, width), F32),
            pltpu.VMEM((2 * S, hid), F32),
            pltpu.VMEM((2 * S, wide), F32),
            pltpu.VMEM((2, 2 * S, wide // 2), BF16),
            pltpu.VMEM((2, 2 * S, wide // 2), BF16),
            pltpu.VMEM((2 * S, wide), F32),
            pltpu.VMEM((2, S, flat // 2), BF16),
            pltpu.VMEM((2, S, flat // 2), BF16),
            pltpu.VMEM((S, flat), F32),
            pltpu.VMEM((S, 16 * width), F32),
            pltpu.VMEM((2 * S, wide), F32),
            pltpu.VMEM((C, 8 * D, width), F32),
            pltpu.VMEM((C, 12 * D, T), BF16),
            pltpu.VMEM((C, 12 * D, T), BF16),
            pltpu.VMEM((2, D, T, T), BF16),
            pltpu.VMEM((D, width, T), BF16),
            pltpu.VMEM((D, 8, C), jnp.int32),
            pltpu.VMEM((C, 4 * D, T), BF16),
            pltpu.VMEM((C, 4 * D, T), BF16),
            pltpu.VMEM((4, T, T), BF16),
            dma((13,)),
            dma((9,)),
            dma((9,)),
            dma((13,)),
            dma((13,)),
        ],
        compiler_params=pltpu.CompilerParams(
            collective_id=0, has_side_effects=True, vmem_limit_bytes=36 * 1024 * 1024
        ),
        name="wukong_step",
    )(
        *(
            pltpu.with_memory_space_constraint(a, pltpu.HBM)
            for a in (
                uniq_rows,
                row_ids.transpose(1, 2, 0),
                sample_idx.T,
                fm_proj.T,
                ln_gain.reshape(1, flat),
                w_up,
                w_down,
                w_lc,
                w_res,
                out_gain.reshape(1, width),
                cotangent,
                moment1.transpose(0, 2, 1),
                moment2,
            )
        )
    )
    layer_out, own, got, m1, m2 = (
        pltpu.with_memory_space_constraint(a, pltpu.VMEM) for a in (layer_out, own, got, m1, m2)
    )
    layer_out, new_moment1, new_moment2, row_step = pl.pallas_call(
        functools.partial(moment_kernel, width),
        out_shape=(
            jax.ShapeDtypeStruct((S, 16 * width), BF16),
            jax.ShapeDtypeStruct((D, width, T), F32),
            jax.ShapeDtypeStruct((D, T), F32),
            jax.ShapeDtypeStruct((D, width, T), F32),
        ),
        in_specs=[vmem] * 5,
        out_specs=(hbm,) * 4,
        scratch_shapes=[
            pltpu.VMEM((D, width, T), F32),
            pltpu.VMEM((D, width, T), F32),
            pltpu.VMEM((D, T), F32),
            dma((2 + 2 * D,)),
        ],
        compiler_params=pltpu.CompilerParams(vmem_limit_bytes=8 * 1024 * 1024),
        name="moments",
    )(layer_out, own, got, m1, m2)
    return (
        layer_out,
        new_moment1.transpose(0, 2, 1),
        new_moment2,
        row_step.transpose(0, 2, 1),
    )


def step(C, R, *args):
    if args[0].shape[1] == 8 and C == 16 and R == 2:
        return fast_body(C, R, *args)
    return plain_body(*args)


def solution(mesh):
    return jax.shard_map(
        functools.partial(step, mesh.shape["col"], mesh.shape["row"]),
        mesh=mesh,
        in_specs=(
            P("row", "col", None),
            P("row", "col", None),
            P("row", "col"),
            P(),
            P(),
            P(None, "row"),
            P("row", None),
            P(),
            P(),
            P(),
            P(("row", "col"), None),
            P("col", "row", None),
            P("col", "row"),
        ),
        out_specs=(
            P(("row", "col"), None),
            P("col", "row", None),
            P("col", "row"),
            P("col", "row", None),
        ),
        check_vma=False,
    )
```

```python
import functools

import jax
import jax.numpy as jnp
from jax import lax
from jax.experimental import pallas as pl
from jax.experimental.pallas import tpu as pltpu
from jax.sharding import PartitionSpec as P

HIGH = lax.Precision.HIGHEST


def layer_norm(values, gain):
    centered = values - jnp.mean(values, -1, keepdims=True)
    inverse = lax.rsqrt(jnp.mean(centered * centered, -1, keepdims=True) + 1e-05)
    normed = centered * inverse
    return (normed * gain, normed, inverse)


def norm_back(grad_out, normed, inverse):
    first = jnp.mean(grad_out, -1, keepdims=True)
    second = jnp.mean(grad_out * normed, -1, keepdims=True)
    return (grad_out - first - normed * second) * inverse


def silu_grad(values):
    sigma = jax.nn.sigmoid(values)
    return sigma * (1.0 + values * (1.0 - sigma))


def plain_body(
    uniq_rows,
    row_ids,
    sample_idx,
    fm_proj,
    ln_gain,
    w_up,
    w_down,
    w_lc,
    w_res,
    out_gain,
    cotangent,
    moment1,
    moment2,
):
    columns = lax.axis_size("col")
    owners = lax.axis_size("row")
    slot_dev = uniq_rows.shape[1]
    width = out_gain.shape[0]
    uniq = uniq_rows.shape[2] // width
    samples = cotangent.shape[0]
    slots = slot_dev * columns
    vocab_dev = moment2.shape[1]
    rank = fm_proj.shape[1]
    fm_rows = w_down.shape[1] // width
    out_rows = w_res.shape[0]
    entry_iota = jnp.arange(uniq, dtype=jnp.int32)
    index_local = sample_idx.reshape(columns, samples, slot_dev)
    index = lax.all_to_all(index_local, "col", split_axis=0, concat_axis=2, tiled=True).reshape(
        samples, slots
    )
    picker = (index[:, :, None] == entry_iota).astype(jnp.bfloat16)
    moved = lax.all_to_all(uniq_rows, "col", split_axis=0, concat_axis=1, tiled=True)
    table = moved.reshape(slots, uniq, width)
    embed = jnp.einsum("stl,tle->ste", picker, table, preferred_element_type=jnp.float32).astype(
        jnp.bfloat16
    )
    compress = jnp.einsum("ste,tk->sek", embed, fm_proj, preferred_element_type=jnp.float32).astype(
        jnp.bfloat16
    )
    gram = jnp.einsum("ste,sek->stk", embed, compress, preferred_element_type=jnp.float32)
    flat = gram.reshape(samples, slots * rank)
    scaled, normed_in, inverse_in = layer_norm(flat, ln_gain)
    normal_in = scaled.astype(jnp.bfloat16)
    hidden_pre = jnp.dot(
        lax.all_gather(normal_in, "row", axis=0, tiled=True),
        w_up,
        preferred_element_type=jnp.float32,
    )
    hidden = jax.nn.silu(hidden_pre).astype(jnp.bfloat16)
    part_rows = hidden
    fm_out = lax.psum_scatter(
        jnp.dot(part_rows, w_down, preferred_element_type=jnp.float32),
        "row",
        scatter_dimension=0,
        tiled=True,
    )
    linear = jnp.einsum("lt,ste->sle", w_lc, embed, preferred_element_type=jnp.float32)
    joined = jnp.concatenate([fm_out.reshape(samples, fm_rows, width), linear], 1)
    normed_out, normed_rows, inverse_rows = layer_norm(joined, out_gain)
    residual = jnp.einsum("ot,ste->soe", w_res, embed, preferred_element_type=jnp.float32)
    layer_out = (normed_out + residual).reshape(samples, out_rows * width).astype(jnp.bfloat16)
    upstream = cotangent.astype(jnp.float32).reshape(samples, out_rows, width)
    grad_joined = norm_back(upstream * out_gain, normed_rows, inverse_rows)
    grad_fm = grad_joined[:, :fm_rows].reshape(samples, fm_rows * width).astype(jnp.bfloat16)
    grad_hidden = lax.dot_general(
        lax.all_gather(grad_fm, "row", axis=0, tiled=True),
        w_down,
        (((1,), (1,)), ((), ())),
        preferred_element_type=jnp.float32,
    )
    grad_pre = (grad_hidden * silu_grad(hidden_pre)).astype(jnp.bfloat16)
    part_rows = grad_pre
    grad_flat = lax.psum_scatter(
        lax.dot_general(
            part_rows, w_up, (((1,), (1,)), ((), ())), preferred_element_type=jnp.float32
        ).astype(jnp.bfloat16),
        "row",
        scatter_dimension=0,
        tiled=True,
    ).astype(jnp.float32)
    grad_gram = norm_back(grad_flat * ln_gain, normed_in, inverse_in).reshape(samples, slots, rank)
    grad_embed = jnp.einsum("stk,sek->ste", grad_gram, compress.astype(jnp.float32), precision=HIGH)
    grad_comp = jnp.einsum(
        "ste,stk->sek", embed, grad_gram, precision=HIGH, preferred_element_type=jnp.float32
    )
    grad_embed = grad_embed + jnp.einsum(
        "tk,sek->ste", fm_proj.astype(jnp.float32), grad_comp, precision=HIGH
    )
    grad_embed = grad_embed + jnp.einsum(
        "lt,sle->ste", w_lc.astype(jnp.float32), grad_joined[:, fm_rows:], precision=HIGH
    )
    grad_embed = grad_embed + jnp.einsum(
        "ot,soe->ste", w_res.astype(jnp.float32), upstream, precision=HIGH
    )
    list_grads = jnp.einsum("stl,ste->tle", picker.astype(jnp.float32), grad_embed, precision=HIGH)
    returned = lax.all_to_all(
        list_grads.reshape(columns, slot_dev, uniq * width),
        "col",
        split_axis=0,
        concat_axis=0,
        tiled=True,
    )
    entry_grads = returned.reshape(columns * slot_dev * uniq, width)
    row_list = row_ids.reshape(-1)
    slot_of = jnp.broadcast_to(
        jnp.arange(slot_dev, dtype=jnp.int32)[None, :, None], row_ids.shape
    ).reshape(-1)
    owner = row_list // vocab_dev
    target = slot_of * vocab_dev + row_list % vocab_dev
    span = slot_dev * vocab_dev
    entries = row_list.shape[0]
    capacity = 5 * entries // (4 * owners)
    onehot = (owner[:, None] == jnp.arange(owners, dtype=jnp.int32)).astype(jnp.int32)
    before = jnp.cumsum(onehot, 0) - onehot
    place = jnp.sum(before * onehot, 1)
    target_slot = owner * capacity + place
    bucket = jnp.zeros((owners * capacity, width), jnp.float32).at[target_slot].set(entry_grads)
    labels = (
        jnp.full((owners * capacity,), -1.0, jnp.float32)
        .at[target_slot]
        .set(target.astype(jnp.float32))
    )
    got_rows, got_labels = (
        lax.all_to_all(
            bucket.reshape(owners, capacity, width), "row", split_axis=0, concat_axis=0, tiled=True
        ),
        lax.all_to_all(
            labels.reshape(owners, capacity), "row", split_axis=0, concat_axis=0, tiled=True
        ),
    )
    segment = jnp.where(got_labels >= 0.0, got_labels, float(span)).astype(jnp.int32).reshape(-1)
    summed = jax.ops.segment_sum(got_rows.reshape(-1, width), segment, num_segments=span + 1)[:span]
    row_grads = summed.reshape(slot_dev, vocab_dev, width)
    new_moment1 = 0.9 * moment1 + 0.1 * row_grads
    new_moment2 = 0.99 * moment2 + 0.01 * jnp.mean(row_grads * row_grads, -1)
    row_step = new_moment1 * lax.rsqrt(new_moment2)[..., None]
    return (layer_out, new_moment1, new_moment2, row_step)


F32 = jnp.float32
BF16 = jnp.bfloat16
NT = (((1,), (1,)), ((), ()))


def iota(shape, dim):
    return lax.broadcasted_iota(jnp.int32, shape, dim)


def matmul(a, b, dims=(((1,), (0,)), ((), ())), precision=None):
    return lax.dot_general(a, b, dims, precision=precision, preferred_element_type=F32)


def fused_kernel(
    C,
    D,
    uniq,
    rid_in,
    sidx_in,
    fmp_in,
    gain_in,
    wup,
    wdn,
    wlc_in,
    wres_in,
    og_in,
    cot_in,
    m1_in,
    m2_in,
    lay_out,
    rg_out,
    pr,
    m1_out,
    m2_out,
    rid,
    sidx,
    fmp,
    gain,
    wlc,
    wres,
    og,
    cot,
    cpeer,
    isend,
    land,
    iland,
    wraw,
    wp,
    wd,
    t32,
    tst,
    lm,
    lmask,
    arep,
    rmat,
    nrm,
    ggr,
    idxn,
    nall,
    y,
    ds,
    c32,
    fsend,
    frecv,
    fm,
    qsend,
    qrecv,
    gq,
    lay32,
    gf32,
    lge,
    sb,
    rland,
    oh,
    ps,
    ridp,
    yb,
    rlandp,
    ohp,
    loc,
    sa,
    ra,
    sx,
    rx,
):
    S, E, U, K, T = 16, 192, 8, 8, 128
    FC, QC = 2, 2
    me = lax.axis_index("col")
    mr = lax.axis_index("row")
    other = 1 - mr

    bits = [1 - 2 * lax.rem(me // (1 << b), 2) for b in range(4)]

    def to_col(i):
        return me + sum(bits[b] * (1 << b) for b in range(4) if i >> b & 1)

    def rcopy(src, dst, ssem, rsem, where):
        return pltpu.make_async_remote_copy(
            src_ref=src,
            dst_ref=dst,
            send_sem=ssem,
            recv_sem=rsem,
            device_id=where,
            device_id_type=pl.DeviceIdType.MESH,
        )

    def row_send(src, dst, sem):
        copy = rcopy(src, dst, sx.at[sem], rx.at[sem], {"row": other})
        copy.start()
        return copy

    barrier = pltpu.get_barrier_semaphore()
    for i in range(1, C):
        pl.semaphore_signal(
            barrier, inc=1, device_id={"col": to_col(i)}, device_id_type=pl.DeviceIdType.MESH
        )
    pl.semaphore_signal(
        barrier, inc=1, device_id={"row": other}, device_id_type=pl.DeviceIdType.MESH
    )
    cp_idx = pltpu.make_async_copy(sidx_in, sidx, loc.at[0])
    cp_idx.start()
    cp_up = pltpu.make_async_copy(wup, wraw, loc.at[1])
    cp_dn = pltpu.make_async_copy(wdn, wd, loc.at[2])
    own_rows = pltpu.make_async_copy(uniq.at[me], land.at[me], loc.at[3])
    own_rows.start()
    small = [
        pltpu.make_async_copy(a, b, loc.at[4 + n])
        for n, (a, b) in enumerate(
            (
                (rid_in, rid),
                (fmp_in, fmp),
                (gain_in, gain),
                (wlc_in, wlc),
                (wres_in, wres),
                (og_in, og),
                (cot_in, cot),
                (m2_in, m2_out),
            )
        )
    ]
    for cp in small:
        cp.start()
    cp_m1 = pltpu.make_async_copy(m1_in, m1_out, loc.at[12])
    cp_up.start()
    cp_dn.start()
    cp_m1.start()
    wide = C * S
    fold_s = ((iota((wide, T), 0) & (S - 1)) == (iota((wide, T), 1) & (S - 1))).astype(F32)
    of_peer = (iota((C, wide), 1) >> 4) == iota((C, wide), 0)
    cp_idx.wait()
    listed = sidx[...].astype(F32)
    spread_d = [
        jnp.where(of_peer, jnp.broadcast_to(listed[d : d + 1, :], (C, wide)), 0.0) for d in range(D)
    ]
    spread_d = matmul(jnp.concatenate(spread_d, 0).astype(BF16), fold_s.astype(BF16))
    spread_d = spread_d.reshape(D, C, T)
    packed = jnp.sum(
        jnp.where((iota((D, C, T), 2) >> 4) == iota((D, C, T), 0), spread_d, 0.0), 0
    ).astype(jnp.int32)
    for p in range(C):
        isend[p] = packed[p : p + 1, :]
    iland[me] = isend[me]
    pl.semaphore_wait(barrier, C)

    order = range(C - 1, 0, -1)
    for i in order:
        p = to_col(i)
        rcopy(isend.at[p], iland.at[me], sa.at[0], ra.at[0], {"col": p}).start()
    for i in order:
        p = to_col(i)
        rcopy(uniq.at[p], land.at[me], sa.at[1], ra.at[1], {"col": p}).start()
    most = pl.ds(0, C - 1)
    all_idx = rcopy(iland.at[most], iland.at[most], sa.at[0], ra.at[0], {"row": other})
    all_rows = rcopy(land.at[most], land.at[most], sa.at[1], ra.at[1], {"row": other})
    c_copy = row_send(cot_in.at[:, pl.ds(0, 8 * E)], cpeer, 0)
    rid_copy = row_send(rid_in, ridp, 12)

    to, at = iota((256, 256), 0), iota((256, 256), 1)
    perm = (((to & 31) * 8 + (to >> 5)) == at).astype(F32).astype(BF16)
    for cp in small:
        cp.wait()
    cp_up.wait()
    for g in range(4):
        blk = matmul(perm, wraw[g * 256 : (g + 1) * 256, :]).astype(BF16)
        for k in range(K):
            wp[k * T + g * 32 : k * T + (g + 1) * 32, :] = blk[k * 32 : (k + 1) * 32, :]
    lane = iota((K, K * T), 1)
    spread = jnp.where((lane & 7) == iota((K, K * T), 0), gain[...], 0.0)
    fold = ((iota((K * T, T), 0) >> 3) == iota((K * T, T), 1)).astype(F32)
    gk = matmul(spread, fold, precision=HIGH)

    amat = jnp.concatenate(
        [
            fmp[...].astype(F32),
            wlc[...].astype(F32),
            wres[...].astype(F32),
        ],
        0,
    )
    for j in range(32):
        arep[j * S : (j + 1) * S, :] = jnp.broadcast_to(amat[j : j + 1, :], (S, T))

    place = (iota((C, T), 0) == (iota((C, T), 1) >> 3)).astype(F32)
    same = iota((D, U, T), 1) == (iota((D, U, T), 2) & (U - 1))

    def labels_of(ids):
        wide = matmul(ids[...].astype(F32).reshape(D * U, C), place, precision=HIGH)
        return jnp.sum(jnp.where(same, wide.reshape(D, U, T), 0.0), 1).astype(jnp.int32)

    labels = labels_of(rid)
    target = iota((T, T), 0)
    for i in range(2):
        local = labels - (mr if i == 0 else other) * T
        for d in range(D):
            oh[i, d] = jnp.where(
                target == jnp.broadcast_to(local[d : d + 1, :], (T, T)), 1.0, 0.0
            ).astype(BF16)

    all_idx.wait_recv()
    group = (iota((D, T), 1) >> 4) == iota((D, T), 0)
    ix = [
        jnp.where(group, jnp.broadcast_to(iland[p].astype(F32), (D, T)), 0.0) for p in range(C)
    ]
    idx_n = matmul(jnp.concatenate(ix, 0).astype(BF16), fold_s[0:T].astype(BF16))
    idxn[...] = idx_n
    idx_t = idx_n.T
    for u in range(U):
        for q in range(4):
            lm[q * T : (q + 1) * T, u * T : (u + 1) * T] = jnp.where(
                idx_t == float(u), arep[q * T : (q + 1) * T, :], 0.0
            ).astype(BF16)
    entry = iota((U, T), 0).astype(F32)

    def fill(src, at, slots=range(0, T, 2)):
        for t in slots:
            rows = [
                jnp.where(
                    jnp.broadcast_to(idxn[v : v + 1, :], (U, T)) == entry,
                    jnp.broadcast_to(src[v : v + 1, :], (U, T)),
                    0.0,
                )
                for v in (t, t + 1)
            ]
            lmask[t // D, t % D * U : (t % D + 2) * U, at * T : (at + 1) * T] = jnp.concatenate(
                rows, 0
            ).astype(BF16)

    for q in range(4):
        ggr[...] = arep[q * T : (q + 1) * T, :].T
        fill(ggr, (q + 3) & 3)
    upstream = cot[...].astype(F32)
    for o in range(16):
        rmat[(8 + o) * S : (9 + o) * S, :] = upstream[:, o * E : (o + 1) * E].astype(BF16)

    rid_copy.wait_recv()
    local = labels_of(ridp) - mr * T
    for d in range(4):
        ohp[d] = jnp.where(
            target == jnp.broadcast_to(local[d + 4 : d + 5, :], (T, T)), 1.0, 0.0
        ).astype(BF16)
    pr[4:D, 0:T, :] = jnp.zeros((4, T, T), BF16)
    own_rows.wait()
    all_rows.wait_recv()
    t32[...] = land[...].astype(F32).reshape(T, U * E)
    for u in range(U):
        tst[u * T : (u + 1) * T, :] = t32[:, u * E : (u + 1) * E].astype(BF16)

    comp = matmul(lm[0:T, :], tst[...]).astype(BF16)
    rmat[512:640, :] = comp
    z = matmul(comp, tst[...], NT)
    gram = jnp.where(idx_t == 0.0, z[:, 0:T], 0.0)
    for u in range(1, U):
        gram = gram + jnp.where(idx_t == float(u), z[:, u * T : (u + 1) * T], 0.0)
    n_flat = float(K * T)
    g3 = gram.reshape(K, S, T)
    mu = jnp.sum(jnp.sum(g3, 0), -1, keepdims=True) / n_flat
    cent = g3 - mu[None]
    inv_in = lax.rsqrt(jnp.sum(jnp.sum(cent * cent, 0), -1, keepdims=True) / n_flat + 1e-05)
    normed_in = cent * inv_in[None]
    nrm[...] = normed_in.reshape(K * S, T)
    for k in range(K):
        nall[0, :, k * T : (k + 1) * T] = (normed_in[k] * gk[k : k + 1, :]).astype(BF16)
    n_copy = row_send(nall.at[0], nall.at[1], 1)

    y[...] = matmul(lm[T:512, :], tst[...])
    gain_out = og[...]
    c_copy.wait_recv()
    c32[0:S, :] = upstream[:, 0 : 8 * E]
    c32[S : 2 * S, :] = cpeer[...].astype(F32)
    up_fm = jnp.concatenate([c32[:, o * E : (o + 1) * E] for o in range(8)], 0) * gain_out
    up_mean = jnp.mean(up_fm, -1, keepdims=True)
    cp_dn.wait()
    n_copy.wait_recv()
    hp = matmul(nall[...].reshape(2 * S, K * T), wp[...])
    sg = jax.nn.sigmoid(hp)
    hid = (hp * sg).astype(BF16)
    f_copies = []
    for c in range(FC):
        cols = slice(c * 8 * E // FC, (c + 1) * 8 * E // FC)
        fp = matmul(hid, wd[:, cols])
        fm[:, cols] = fp
        fsend[c, 0:S] = fp[S : 2 * S].astype(BF16)
        fsend[c, S : 2 * S] = fp[0:S].astype(BF16)
        f_copies.append(row_send(fsend.at[c], frecv.at[c], 2 + c))
    ds[...] = sg * (1.0 + hp * (1.0 - sg))

    def out_norm(joined, o):
        up = upstream[:, o * E : (o + 1) * E]
        c = joined - jnp.mean(joined, -1, keepdims=True)
        inv = lax.rsqrt(jnp.mean(c * c, -1, keepdims=True) + 1e-05)
        nr = c * inv
        return nr, norm_back(up * gain_out, nr, inv)

    for o in range(8, 16):
        nr, gj = out_norm(y[(o - 8) * S : (o - 7) * S, :], o)
        lay32[:, o * E : (o + 1) * E] = nr * gain_out + y[(8 + o) * S : (9 + o) * S, :]
        rmat[(o - 8) * S : (o - 7) * S, :] = gj.astype(BF16)

    normed_fm, gh = [], None
    per = 8 // FC
    for c in range(FC):
        f_copies[c].wait_recv()
        cols = slice(c * per * E, (c + 1) * per * E)
        rows = slice(c * per * 2 * S, (c + 1) * per * 2 * S)
        fm[:, cols] += frecv[c].astype(F32)
        joined = jnp.concatenate(
            [fm[:, o * E : (o + 1) * E] for o in range(c * per, (c + 1) * per)], 0
        )
        cen = joined - jnp.mean(joined, -1, keepdims=True)
        inv_fm = lax.rsqrt(jnp.mean(cen * cen, -1, keepdims=True) + 1e-05)
        normed = cen * inv_fm
        across = jnp.mean(up_fm[rows] * cen, -1, keepdims=True) * inv_fm
        grad_fm = (up_fm[rows] - up_mean[rows] - normed * across) * inv_fm
        for o in range(per):
            at = (c * per + o) * E
            gf32[:, at : at + E] = grad_fm[o * 2 * S : (o + 1) * 2 * S]
            normed_fm.append(normed[o * 2 * S : o * 2 * S + S])
        part = matmul(gf32[:, cols].astype(BF16), wd[:, cols], NT)
        gh = part if gh is None else gh + part
    gp = (gh * ds[...]).astype(BF16)
    q_copies = []
    for c in range(QC):
        cols = slice(c * K * T // QC, (c + 1) * K * T // QC)
        part = matmul(gp, wp[cols, :], NT)
        gq[:, cols] = part[0:S]
        qsend[c] = part[S : 2 * S].astype(BF16)
        q_copies.append(row_send(qsend.at[c], qrecv.at[c], 2 + FC + c))
    for o in range(8):
        lay32[:, o * E : (o + 1) * E] = (
            normed_fm[o] * gain_out + y[(8 + o) * S : (9 + o) * S, :]
        )
    lay_out[...] = lay32[...].astype(BF16)
    lge[...] = matmul(
        lmask[:, :, 0:384].reshape(C * D * U, 384), rmat[0:384, :]
    ).reshape(C, D * U, E)
    for c in range(QC):
        q_copies[c].wait_recv()
    width = K // QC
    qs = [
        (
            gq[:, k * T : (k + 1) * T]
            + qrecv[k // width, :, k % width * T : (k % width + 1) * T].astype(F32)
        )
        * gk[k : k + 1, :]
        for k in range(K)
    ]
    ns = [nrm[k * S : (k + 1) * S, :] for k in range(K)]
    first = jnp.sum(sum(qs), -1, keepdims=True) / n_flat
    second = jnp.sum(sum(q * n for q, n in zip(qs, ns)), -1, keepdims=True) / n_flat
    for k in range(K):
        ggr[k * S : (k + 1) * S, :] = (qs[k] - first - ns[k] * second) * inv_in
    gg = ggr[...]
    for u in range(U):
        lm[0:T, u * T : (u + 1) * T] = jnp.where(idx_t == float(u), gg, 0.0).astype(BF16)
    ggr[...] = gg.T
    rmat[384:512, :] = matmul(lm[0:T, :], tst[...]).astype(BF16)

    units = []

    def col_send(src, dst, sem):
        for i in order:
            p = to_col(i)
            rcopy(src(p), dst, sa.at[sem], ra.at[sem], {"col": p}).start()

    def unit_send(j, row):
        cut = pl.ds(row, 16)
        col_send(lambda p: sb.at[p, cut], rland.at[me, cut], 2 + j)
        units.append(
            rcopy(
                sb.at[most, cut], rland.at[most, cut], sa.at[2 + j], ra.at[2 + j], {"row": other}
            )
        )

    y_copies = []
    for half in (1, 0):
        at = half * 32
        fill(ggr, 4, [t for t in range(0, T, 2) if t % D // 4 == half])
        part = matmul(lmask[:, at : at + 32, 384:640].reshape(C * 32, 256), rmat[384:640, :])
        part = part.reshape(C, 32, E) + lge[:, at : at + 32, :]
        row = half * 48
        top = part[:, :, T:E]
        sb[:, row : row + 16, :] = jnp.concatenate([top[:, :16], top[:, 16:]], -1).astype(BF16)
        sb[:, row + 16 : row + 48, :] = part[:, :, 0:T].astype(BF16)
        if half:
            for c in range(2):
                y_copies.append(
                    row_send(
                        sb.at[:, pl.ds(64 + c * 16, 16)], yb.at[:, pl.ds(c * 16, 16)], 10 + c
                    )
                )
            unit_send(0, 48)
        else:
            for j in range(3):
                unit_send(1 + j, j * 16)
    late = pl.ds(64, 32)
    col_send(lambda p: sb.at[p, late], rland.at[me, late], 6)
    lists = [
        rcopy(sb.at[most, late], rland.at[most, late], sa.at[6], ra.at[6], {"row": other})
    ]
    rland[me] = sb[me]

    def relay(c):
        y_copies[c].wait_recv()
        cut = pl.ds(c * 16, 16)
        col_send(lambda p: yb.at[p, cut], rlandp.at[me, cut], 7 + c)
        rlandp[me, c * 16 : (c + 1) * 16, :] = yb[me, c * 16 : (c + 1) * 16, :]
        lists.append(
            rcopy(yb.at[most, cut], rlandp.at[most, cut], sa.at[7 + c], ra.at[7 + c], {"row": other})
        )

    def halves(ref, row):
        both = ref[:, row : row + 16, :].astype(F32)
        return [both[:, h * U : (h + 1) * U, :].reshape(T, T).T.astype(BF16) for h in range(2)]

    p_copies = []
    for j in range(4):
        if j < 2:
            relay(j)
        units[j].wait_recv()
        base, row = ((4, 48), (0, 0), (0, 16), (2, 32))[j]
        pieces = []
        for h, x in enumerate(halves(rland, row)):
            if j < 2:
                pieces.append((base + h, T, E, x[: E - T]))
                pieces.append((base + 2 + h, T, E, x[E - T :]))
            else:
                pieces.append((base + h, 0, T, x))
        for d, a, b, x in pieces:
            ps[d, a:b, :] = matmul(x, oh[1, d], NT).astype(BF16)
        part = (pl.ds(base, 4), pl.ds(T, E - T)) if j < 2 else (pl.ds(base, 2), pl.ds(0, T))
        p_copies.append(row_send(ps.at[part], pr.at[part], 2 + FC + QC + j))
        for d, a, b, x in pieces:
            rg_out[d, a:b, :] = matmul(x, oh[0, d], NT)
    lists[0].wait_recv()
    for c in range(2):
        for h, x in enumerate(halves(rland, 64 + c * 16)):
            d = 4 + 2 * c + h
            rg_out[d, 0:T, :] = matmul(x, oh[0, d], NT)
    for c in range(2):
        lists[1 + c].wait_recv()
        for h, x in enumerate(halves(rlandp, c * 16)):
            d = 4 + 2 * c + h
            rg_out[d, 0:T, :] += matmul(x, ohp[d - 4], NT)
    cp_m1.wait()
    for cp in p_copies:
        cp.wait_recv()
    for cp in (
        all_idx,
        all_rows,
        c_copy,
        n_copy,
        *f_copies,
        *q_copies,
        rid_copy,
        *units,
        *y_copies,
        *lists,
        *p_copies,
    ):
        cp.wait_send()


def moment_kernel(
    width, lay, own, got, m1, m2, lay_out, m1_out, m2_out, step_out, mv, sv, m2v, sem
):
    D = own.shape[0]
    copies = [pltpu.make_async_copy(lay, lay_out, sem.at[0])]
    copies[0].start()
    for d in range(D):
        g = own[d] + got[d].astype(F32)
        first = 0.9 * m1[d] + 0.1 * g
        second = 0.99 * m2[d : d + 1, :] + 0.01 * (jnp.sum(g * g, 0, keepdims=True) / width)
        mv[d] = first
        m2v[d : d + 1, :] = second
        sv[d] = first * lax.rsqrt(second)
        for n, (a, b) in enumerate(((mv, m1_out), (sv, step_out))):
            copies.append(pltpu.make_async_copy(a.at[d], b.at[d], sem.at[2 + 2 * d + n]))
            copies[-1].start()
    copies.append(pltpu.make_async_copy(m2v, m2_out, sem.at[1]))
    copies[-1].start()
    for cp in copies:
        cp.wait()


def fast_body(
    C,
    R,
    uniq_rows,
    row_ids,
    sample_idx,
    fm_proj,
    ln_gain,
    w_up,
    w_down,
    w_lc,
    w_res,
    out_gain,
    cotangent,
    moment1,
    moment2,
):
    D = uniq_rows.shape[1]
    S = cotangent.shape[0]
    hid = w_up.shape[1]
    wide = w_down.shape[1]
    flat = w_up.shape[0]
    width = out_gain.shape[0]
    T = C * D
    vmem = pl.BlockSpec(memory_space=pltpu.VMEM)
    hbm = pl.BlockSpec(memory_space=pl.ANY)
    dma = pltpu.SemaphoreType.DMA
    layer_out, own, got, m1, m2 = pl.pallas_call(
        functools.partial(fused_kernel, C, D),
        out_shape=(
            pltpu.VMEM((S, 16 * width), BF16),
            pltpu.VMEM((D, width, T), F32),
            pltpu.VMEM((D, width, T), BF16),
            pltpu.VMEM((D, width, T), F32),
            pltpu.VMEM((D, T), F32),
        ),
        in_specs=[hbm] * 13,
        out_specs=(vmem,) * 5,
        scratch_shapes=[
            pltpu.VMEM((D, 8, C), jnp.int32),
            pltpu.VMEM((D, C * S), jnp.int32),
            pltpu.VMEM((8, T), BF16),
            pltpu.VMEM((1, flat), F32),
            pltpu.VMEM((8, T), BF16),
            pltpu.VMEM((16, T), BF16),
            pltpu.VMEM((1, width), F32),
            pltpu.VMEM((S, 16 * width), BF16),
            pltpu.VMEM((S, wide), BF16),
            pltpu.VMEM((C, 1, T), jnp.int32),
            pltpu.VMEM((C, D, wide), BF16),
            pltpu.VMEM((C, 1, T), jnp.int32),
            pltpu.VMEM((flat, hid), BF16),
            pltpu.VMEM((flat, hid), BF16),
            pltpu.VMEM((hid, wide), BF16),
            pltpu.VMEM((T, wide), F32),
            pltpu.VMEM((8 * T, width), BF16),
            pltpu.VMEM((512, 8 * T), BF16),
            pltpu.VMEM((C, 8 * D, 640), BF16),
            pltpu.VMEM((512, T), F32),
            pltpu.VMEM((640, width), BF16),
            pltpu.VMEM((128, T), F32),
            pltpu.VMEM((128, T), F32),
            pltpu.VMEM((T, 128), F32),
            pltpu.VMEM((2, S, flat), BF16),
            pltpu.VMEM((384, width), F32),
            pltpu.VMEM((2 * S, hid), F32),
            pltpu.VMEM((2 * S, wide), F32),
            pltpu.VMEM((2, 2 * S, wide // 2), BF16),
            pltpu.VMEM((2, 2 * S, wide // 2), BF16),
            pltpu.VMEM((2 * S, wide), F32),
            pltpu.VMEM((2, S, flat // 2), BF16),
            pltpu.VMEM((2, S, flat // 2), BF16),
            pltpu.VMEM((S, flat), F32),
            pltpu.VMEM((S, 16 * width), F32),
            pltpu.VMEM((2 * S, wide), F32),
            pltpu.VMEM((C, 8 * D, width), F32),
            pltpu.VMEM((C, 12 * D, T), BF16),
            pltpu.VMEM((C, 12 * D, T), BF16),
            pltpu.VMEM((2, D, T, T), BF16),
            pltpu.VMEM((D, width, T), BF16),
            pltpu.VMEM((D, 8, C), jnp.int32),
            pltpu.VMEM((C, 4 * D, T), BF16),
            pltpu.VMEM((C, 4 * D, T), BF16),
            pltpu.VMEM((4, T, T), BF16),
            dma((13,)),
            dma((9,)),
            dma((9,)),
            dma((13,)),
            dma((13,)),
        ],
        compiler_params=pltpu.CompilerParams(
            collective_id=0, has_side_effects=True, vmem_limit_bytes=36 * 1024 * 1024
        ),
        name="wukong_step",
    )(
        *(
            pltpu.with_memory_space_constraint(a, pltpu.HBM)
            for a in (
                uniq_rows,
                row_ids.transpose(1, 2, 0),
                sample_idx.T,
                fm_proj.T,
                ln_gain.reshape(1, flat),
                w_up,
                w_down,
                w_lc,
                w_res,
                out_gain.reshape(1, width),
                cotangent,
                moment1.transpose(0, 2, 1),
                moment2,
            )
        )
    )
    layer_out, own, got, m1, m2 = (
        pltpu.with_memory_space_constraint(a, pltpu.VMEM) for a in (layer_out, own, got, m1, m2)
    )
    layer_out, new_moment1, new_moment2, row_step = pl.pallas_call(
        functools.partial(moment_kernel, width),
        out_shape=(
            jax.ShapeDtypeStruct((S, 16 * width), BF16),
            jax.ShapeDtypeStruct((D, width, T), F32),
            jax.ShapeDtypeStruct((D, T), F32),
            jax.ShapeDtypeStruct((D, width, T), F32),
        ),
        in_specs=[vmem] * 5,
        out_specs=(hbm,) * 4,
        scratch_shapes=[
            pltpu.VMEM((D, width, T), F32),
            pltpu.VMEM((D, width, T), F32),
            pltpu.VMEM((D, T), F32),
            dma((2 + 2 * D,)),
        ],
        compiler_params=pltpu.CompilerParams(vmem_limit_bytes=8 * 1024 * 1024),
        name="moments",
    )(layer_out, own, got, m1, m2)
    return (
        layer_out,
        new_moment1.transpose(0, 2, 1),
        new_moment2,
        row_step.transpose(0, 2, 1),
    )


def step(C, R, *args):
    if args[0].shape[1] == 8 and C == 16 and R == 2:
        return fast_body(C, R, *args)
    return plain_body(*args)


def solution(mesh):
    return jax.shard_map(
        functools.partial(step, mesh.shape["col"], mesh.shape["row"]),
        mesh=mesh,
        in_specs=(
            P("row", "col", None),
            P("row", "col", None),
            P("row", "col"),
            P(),
            P(),
            P(None, "row"),
            P("row", None),
            P(),
            P(),
            P(),
            P(("row", "col"), None),
            P("col", "row", None),
            P("col", "row"),
        ),
        out_specs=(
            P(("row", "col"), None),
            P("col", "row", None),
            P("col", "row"),
            P("col", "row", None),
        ),
        check_vma=False,
    )
```
